32 devices in a mesh: groups: 2 (over y), feat: 4 (over z), tok: 2 (over x), rep: 2 (over core).
Axes of the slice: x: 2, y: 2, z: 4, core: 2. Of those that a mesh axis runs over, the one named last changes fastest.
Arguments:
- tokens: bfloat16 [448, 8192], P(('groups', 'tok', 'rep'), 'feat'), parts along dimension 0, may hold values from -6 to 6
- gate_weight: bfloat16 [8192, 14336], P('feat', ('tok', 'rep')), may hold values from -0.09375 to 0.09375
- up_weight: bfloat16 [8192, 14336], P('feat', ('tok', 'rep')), may hold values from -0.09375 to 0.09375
- down_weight: bfloat16 [14336, 8192], P(('tok', 'rep'), 'feat'), may hold values from -0.0625 to 0.0625
- gate_mask: int32 [64, 112], P('feat', ('tok', 'rep')), may hold values 0 or 1
- up_mask: int32 [64, 112], P('feat', ('tok', 'rep')), may hold values 0 or 1
- down_mask: int32 [112, 64], P(('tok', 'rep'), 'feat'), may hold values 0 or 1
Outputs:
- mixed: bfloat16 [448, 8192], P(('groups', 'tok', 'rep'), 'feat'), parts along dimension 0
The draws below stay inside these ranges and needn't reach their ends.
There are 2 independent parts, one for each index of `groups`. The reference program is written for one: setup_inputs(seed, part) draws one part's arguments, and reference() takes and returns one part's arrays. A program takes and returns all parts, laid end to end along the dimension named above; an argument that names none is the same for every part. Nothing has to cross between parts.
Inputs may be any that keep to these rules, and one draw needn't show every extreme that they name: `gate_mask`: entries are 0 or 1; 1 keeps the block. `up_mask`: entries are 0 or 1; 1 keeps the block. `down_mask`: entries are 0 or 1; 1 keeps the block.
All inputs are finite; a program needn't handle non-finite values.
Results may differ from the reference program's by a relative error of at most 0.02.
Values may be sent and summed in bfloat16 or wider, within the bound.
A program may use at most 192 MiB of HBM per device.

```python
import jax
import jax.numpy as jnp
from jax import lax

D = 8192
HID = 14336
BLOCK = 128
TOKENS = 224
N_FEAT = 4
N_TOK = 2
N_REP = 2


def plant(array, own_key, low, top_value):
    spot = [jax.random.randint(jax.random.fold_in(own_key, axis), (), 0, length) for axis, length in enumerate(array.shape)]
    main_axis = array.shape.index(max(array.shape))
    beside = spot[:main_axis] + [(spot[main_axis] + 1) % array.shape[main_axis]] + spot[main_axis + 1:]
    return array.at[tuple(spot)].set(low).at[tuple(beside)].set(top_value)


def shard_levels(key, extent, shards, least, high):
    def one(axis_at, parts):
        steps = jax.random.uniform(jax.random.fold_in(jax.random.fold_in(key, 6), axis_at), (parts,), jnp.float32, least / len(shards), high / len(shards))
        return jnp.repeat(jnp.exp(steps), extent[axis_at] // parts).reshape((-1,) + (1,) * (len(extent) - axis_at - 1))

    loudness = one(*shards[0])
    for cut in shards[1:]:
        loudness = loudness * one(*cut)
    return loudness


def noise(rng, extent, deviation, limit, shards=(), dtype=jnp.bfloat16):
    gain = shard_levels(rng, extent, shards, -0.22, 0.18) if shards else 1.0
    entries = jax.random.normal(rng, extent, jnp.float32) * deviation * gain
    return jnp.minimum(jnp.maximum(entries, -limit), limit).astype(dtype)


def setup_inputs(seed: int = 0, part: int = 0) -> dict:
    seeds = jax.random.split(jax.random.key(seed), 8)
    part_splits = jax.random.split(jax.random.fold_in(seeds[7], part), 8)
    return {
        "tokens": noise(part_splits[0], (TOKENS, D), 1.0, 6.0, ((0, 4), (1, 4))),
        "gate_weight": noise(seeds[1], (D, HID), (D // 2) ** -0.5, 0.09375, ((0, 4), (1, 4))),
        "up_weight": noise(seeds[2], (D, HID), (D // 2) ** -0.5, 0.09375, ((0, 4), (1, 4))),
        "down_weight": noise(seeds[3], (HID, D), (HID // 2) ** -0.5, 0.0625, ((0, 4), (1, 4))),
        "gate_mask": plant((jax.random.randint(seeds[4], (D // BLOCK, HID // BLOCK), 0, 2) < 1).astype(jnp.int32), jax.random.fold_in(seeds[4], 1), 0, 1),
        "up_mask": plant((jax.random.randint(seeds[5], (D // BLOCK, HID // BLOCK), 0, 2) < 1).astype(jnp.int32), jax.random.fold_in(seeds[5], 1), 0, 1),
        "down_mask": plant((jax.random.randint(seeds[6], (HID // BLOCK, D // BLOCK), 0, 2) < 1).astype(jnp.int32), jax.random.fold_in(seeds[6], 1), 0, 1),
    }


def expand(mask_grid):
    return jnp.repeat(jnp.repeat(mask_grid.astype(jnp.bfloat16), BLOCK, 0), BLOCK, 1)


def reference(tokens, gate_weight, up_weight, down_weight, gate_mask, up_mask, down_mask):
    gate_kept = gate_weight * expand(gate_mask)
    up_kept = up_weight * expand(up_mask)
    down_kept = down_weight * expand(down_mask)
    feature_cols = D // N_FEAT
    gate = jnp.zeros((TOKENS, HID), jnp.float32)
    up_sum = jnp.zeros((TOKENS, HID), jnp.float32)
    for segment in range(N_FEAT):
        lower = segment * feature_cols
        inputs = tokens[:, lower:lower + feature_cols]
        gate_part = jnp.dot(inputs, gate_kept[lower:lower + feature_cols], preferred_element_type=jnp.float32)
        up_part = jnp.dot(inputs, up_kept[lower:lower + feature_cols], preferred_element_type=jnp.float32)
        gate = gate + lax.optimization_barrier(gate_part.astype(jnp.bfloat16)).astype(jnp.float32)
        up_sum = up_sum + lax.optimization_barrier(up_part.astype(jnp.bfloat16)).astype(jnp.float32)
    hidden = (jax.nn.silu(gate) * up_sum).astype(jnp.bfloat16)
    hidden_cols = HID // (N_TOK * N_REP)
    output = jnp.zeros((TOKENS, D), jnp.float32)
    for segment in range(N_TOK * N_REP):
        lower = segment * hidden_cols
        down_part = jnp.dot(hidden[:, lower:lower + hidden_cols], down_kept[lower:lower + hidden_cols], preferred_element_type=jnp.float32)
        output = output + lax.optimization_barrier(down_part.astype(jnp.bfloat16)).astype(jnp.float32)
    return output.astype(jnp.bfloat16)
```

```python
import functools

import jax
import jax.numpy as jnp
from jax import lax
from jax.experimental import pallas as pl
from jax.experimental.pallas import tpu as pltpu
from jax.sharding import PartitionSpec as P

BLOCK = 128
HOP = 3
BACK = 3
LEAD = 2
SLACK = 2
EARLY = 5
MESH = pl.DeviceIdType.MESH


def kernel(nf, nx, nr, tokens, gate_w, up_w, down_w, gate_m, up_m, down_m, out,
           arrived, tok, wgu, wd, sums, part, taken, hid, acc, leaving, coming,
           tok_send, tok_recv, own_sem, g_sem, u_sem, d_sem, part_send, part_recv,
           hid_send, hid_recv, out_send, out_recv):
    z, x, r = lax.axis_index("feat"), lax.axis_index("tok"), lax.axis_index("rep")
    rows = arrived.shape[1]
    feats = tok.shape[2]
    chunks = wgu.shape[0]
    width = wd.shape[1]
    up_chunks, down_chunks = (chunks + 1) // 2, chunks // 2
    early = min(EARLY, down_chunks)
    peers = [(g, q) for g in range(nx) for q in range(nr)]

    def chip(g):
        return lax.rem(x + 1 + g, nx)

    barrier = pltpu.get_barrier_semaphore()
    for g in range(nx - 1):
        for q in range(nr):
            pl.semaphore_signal(barrier, inc=1, device_id={"tok": chip(g), "rep": q}, device_id_type=MESH)
    for step in range(1, nr):
        pl.semaphore_signal(barrier, inc=1, device_id={"rep": lax.rem(r + step, nr)}, device_id_type=MESH)

    @pl.when(z > 0)
    def _():
        pl.semaphore_signal(barrier, inc=1, device_id={"feat": z - 1}, device_id_type=MESH)

    @pl.when(z < nf - 1)
    def _():
        pl.semaphore_signal(barrier, inc=1, device_id={"feat": z + 1}, device_id_type=MESH)

    def gate_copy(j):
        cols = pl.ds(pl.multiple_of(j * width, width), width)
        return pltpu.make_async_copy(gate_w.at[:, cols], wgu.at[j, :, pl.ds(0, width)], g_sem.at[j])

    def up_copy(j):
        cols = pl.ds(pl.multiple_of(j * width, width), width)
        return pltpu.make_async_copy(up_w.at[:, cols], wgu.at[j, :, pl.ds(width, width)], u_sem.at[j])

    def down_copy(j):
        at = pl.ds(pl.multiple_of(j * width, width), width)
        return pltpu.make_async_copy(down_w.at[at, :], wd.at[j], d_sem.at[j])

    own_copy = pltpu.make_async_copy(tokens, arrived.at[(nx - 1) * nr + r], own_sem)
    own_copy.start()

    lead = min(LEAD, down_chunks)
    for c in range(lead):
        for e in range(2):
            j = jnp.where((z <= nf - 1 - z) == (e == 0), 0, up_chunks) + c
            gate_copy(j).start()
            up_copy(j).start()
    acc[...] = jnp.zeros_like(acc)

    ends = (z == 0).astype(jnp.int32) + (z == nf - 1).astype(jnp.int32)
    pl.semaphore_wait(barrier, nx * nr + 1 - ends)

    def near_copy(step):
        return pltpu.make_async_remote_copy(
            src_ref=tokens, dst_ref=arrived.at[(nx - 1) * nr + r],
            send_sem=tok_send.at[(nx - 1) * nr + step], recv_sem=tok_recv.at[(nx - 1) * nr + r],
            device_id={"rep": lax.rem(r + step, nr)}, device_id_type=MESH)

    def far_copy(g, q):
        slot = (nx - 2 - g) * nr + r
        return pltpu.make_async_remote_copy(
            src_ref=tokens, dst_ref=arrived.at[slot],
            send_sem=tok_send.at[g * nr + q], recv_sem=tok_recv.at[slot],
            device_id={"tok": chip(g), "rep": q}, device_id_type=MESH)

    def landed(slot):
        pltpu.make_async_remote_copy(
            src_ref=tokens, dst_ref=arrived.at[slot],
            send_sem=tok_send.at[0], recv_sem=tok_recv.at[slot],
            device_id={"rep": lax.rem(r + 1, nr)}, device_id_type=MESH).wait_recv()

    for step in range(1, nr):
        near_copy(step).start()
    for g in range(nx - 1):
        for q in range(nr):
            far_copy(g, q).start()
    own_copy.wait()
    for step in range(1, nr):
        landed((nx - 1) * nr + lax.rem(r + step, nr))
    for q in range(nr):
        tok[nx - 1, q * rows:(q + 1) * rows, :] = arrived[(nx - 1) * nr + q]

    def place(d):
        p = jnp.where(d == 0, z, nf - 1 - z)
        count = up_chunks if up_chunks == down_chunks else jnp.where(d == 0, up_chunks, down_chunks)
        return p, count, nx * count

    def unit(u, d, count):
        mine = (u < early) | (u >= early + (nx - 1) * count)
        other = jnp.maximum(u - early, 0)
        group = jnp.where(mine, nx - 1, other // count)
        c = jnp.where(u < early, u, jnp.where(mine, u - (nx - 1) * count, other % count))
        first = (u < early) | ((u >= 2 * early) & (u < early + count))
        return group, d * up_chunks + c, first

    def ahead(d):
        return z + 1 - 2 * d

    def behind(d):
        return z - 1 + 2 * d

    def hidden_unit(h, count):
        others = (nx - 1) * count
        c = h - others
        return jnp.where(c < 0, early + h, jnp.where(c < early, c, h))

    def part_copy(d, u, m):
        return pltpu.make_async_remote_copy(
            src_ref=part.at[d, u, m], dst_ref=taken.at[d, u, m],
            send_sem=part_send.at[d, u, m], recv_sem=part_recv.at[d, u, m],
            device_id={"feat": ahead(d)}, device_id_type=MESH)

    def hid_copy(d, u):
        return pltpu.make_async_remote_copy(
            src_ref=hid.at[d, u], dst_ref=hid.at[d, u],
            send_sem=hid_send.at[d, u], recv_sem=hid_recv.at[d, u],
            device_id={"feat": behind(d)}, device_id_type=MESH)

    def splat(scalar, shape):
        return jnp.full(shape, scalar.astype(jnp.float32)).astype(jnp.bfloat16)

    others = (nx - 1) * up_chunks
    begin = HOP * (nf - 1) + max(nr * (early + others) - others, (nr - 1) * nx * up_chunks) + SLACK

    def multiply(k, d):
        p, count, units = place(d)
        t = k - HOP * p + nr
        u = t // nr

        @pl.when((t >= 0) & (u < units) & (t % nr == 0))
        def _():
            group, j, first = unit(u, d, count)

            @pl.when(u + lead < count)
            def _():
                gate_copy(d * up_chunks + u + lead).start()
                up_copy(d * up_chunks + u + lead).start()

            below = u - (count - lead if nx > 1 else 0)

            @pl.when((below >= 0) & (below < count))
            def _():
                down_copy(d * up_chunks + below).start()

            @pl.when(first)
            def _():
                gate_copy(j).wait()
                up_copy(j).wait()

            total = None
            deep = 2 * BLOCK if feats % (2 * BLOCK) == 0 else BLOCK
            for lo in range(0, feats, deep):
                tall = []
                for b in range(lo // BLOCK, (lo + deep) // BLOCK):
                    wide = []
                    for n in range(2 * width // BLOCK):
                        mask = gate_m if n < width // BLOCK else up_m
                        keep = mask[b, j * (width // BLOCK) + n % (width // BLOCK)]
                        wide.append(wgu[j, b * BLOCK:(b + 1) * BLOCK, n * BLOCK:(n + 1) * BLOCK] * splat(keep, (BLOCK, BLOCK)))
                    tall.append(jnp.concatenate(wide, axis=1))
                product = jnp.dot(tok[group, :, lo:lo + deep], jnp.concatenate(tall, axis=0),
                                  preferred_element_type=jnp.float32)
                total = product if total is None else total + product
            for m in range(nr):
                sums[d, u % 2, m] = total[m * rows:(m + 1) * rows, :]

    def reduce(k, d):
        p, count, units = place(d)
        t = k - HOP * p
        u, m = t // nr, t % nr

        @pl.when((t >= 0) & (u < units))
        def _():
            here = sums.at[d, u % 2, m]

            @pl.when(p > 0)
            def _():
                part_copy(d, u, m).wait_recv()
                here[...] += taken[d, u, m].astype(jnp.float32)

            @pl.when(p < nf - 1)
            def _():
                part[d, u, m] = here[...].astype(jnp.bfloat16)
                part_copy(d, u, m).start()

            for s in range(nr):
                @pl.when((p == nf - 1) & (m == s))
                def _():
                    gate, up = here[:, :width], here[:, width:]
                    hid[d, u, s * rows:(s + 1) * rows, :] = (gate / (1.0 + jnp.exp(-gate)) * up).astype(jnp.bfloat16)

    def spread(k, d):
        p, count, units = place(d)
        h = k - begin - BACK * (nf - 1 - p)

        @pl.when((h >= 0) & (h < units))
        def _():
            u = hidden_unit(h, count)
            group, j, _ = unit(u, d, count)

            @pl.when(p < nf - 1)
            def _():
                hid_copy(d, u).wait_recv()

            @pl.when(p > 0)
            def _():
                hid_copy(d, u).start()

            @pl.when(h < count)
            def _():
                down_copy(j).wait()

            for n in range(wd.shape[2] // BLOCK // 2):
                cols = slice(2 * n * BLOCK, 2 * (n + 1) * BLOCK)
                tall = []
                for b in range(width // BLOCK):
                    wide = []
                    for m in (2 * n, 2 * n + 1):
                        keep = down_m[m, j * (width // BLOCK) + b]
                        wide.append(wd[j, b * BLOCK:(b + 1) * BLOCK, m * BLOCK:(m + 1) * BLOCK] * splat(keep, (BLOCK, BLOCK)))
                    tall.append(jnp.concatenate(wide, axis=1))
                acc[group, :, cols] += jnp.dot(hid[d, u], jnp.concatenate(tall, axis=0),
                                               preferred_element_type=jnp.float32)

    def out_copy(g, q):
        slot = g * nr + r
        return pltpu.make_async_remote_copy(
            src_ref=leaving.at[g * nr + q], dst_ref=coming.at[slot],
            send_sem=out_send.at[g * nr + q], recv_sem=out_recv.at[slot],
            device_id={"tok": chip(g), "rep": q}, device_id_type=MESH)

    def last_copy(step):
        return pltpu.make_async_remote_copy(
            src_ref=leaving.at[(nx - 1) * nr + step], dst_ref=coming.at[(nx - 1) * nr + r],
            send_sem=out_send.at[(nx - 1) * nr + step], recv_sem=out_recv.at[(nx - 1) * nr + r],
            device_id={"rep": lax.rem(r + step, nr)}, device_id_type=MESH)

    starts = HOP * jnp.minimum(z, nf - 1 - z) + nr * early - nr
    flip = (z > nf - 1 - z).astype(jnp.int32)

    @pl.loop(-nr, begin + BACK * (nf - 1) + nx * up_chunks)
    def _(k):
        @pl.loop(0, 2)
        def _(e):
            reduce(k, (e + flip) % 2)

        @pl.when(k == starts)
        def _():
            for g in range(nx - 1):
                for q in range(nr):
                    landed(g * nr + q)
                    tok[g, q * rows:(q + 1) * rows, :] = arrived[g * nr + q]

        @pl.loop(0, 2)
        def _(e):
            multiply(k, (e + flip) % 2)

        @pl.loop(0, 2)
        def _(e):
            spread(k, (e + flip) % 2)

        for g in range(nx - 1):
            ends = [begin + BACK * (nf - 1 - p) + (g + 1) * count - 1
                    for count, p in ((up_chunks, z), (down_chunks, nf - 1 - z))]

            @pl.when(k == jnp.maximum(*ends))
            def _():
                for q in range(nr):
                    leaving[g * nr + q] = acc[g, q * rows:(q + 1) * rows, :].astype(jnp.bfloat16)
                    out_copy(g, q).start()

    for step in range(1, nr):
        at = pl.ds(pl.multiple_of(lax.rem(r + step, nr) * rows, 8), rows)
        leaving[(nx - 1) * nr + step] = acc[nx - 1, at, :].astype(jnp.bfloat16)
        last_copy(step).start()
    final = acc[nx - 1, pl.ds(pl.multiple_of(r * rows, 8), rows), :]

    def summed(slot):
        pltpu.make_async_remote_copy(
            src_ref=leaving.at[0], dst_ref=coming.at[slot],
            send_sem=out_send.at[0], recv_sem=out_recv.at[slot],
            device_id={"rep": lax.rem(r + 1, nr)}, device_id_type=MESH).wait_recv()
        return coming[slot].astype(jnp.float32)

    for slot in range((nx - 1) * nr):
        final += summed(slot)
    for step in range(1, nr):
        final += summed((nx - 1) * nr + lax.rem(r + step, nr))
    out[...] = final.astype(out.dtype)

    for step in range(1, nr):
        near_copy(step).wait_send()
        last_copy(step).wait_send()
    for g in range(nx - 1):
        for q in range(nr):
            far_copy(g, q).wait_send()
            out_copy(g, q).wait_send()

    @pl.loop(0, 2)
    def _(d):
        p, count, units = place(d)

        @pl.loop(0, nx * up_chunks)
        def _(u):
            @pl.when((u < units) & (p < nf - 1))
            def _():
                for m in range(nr):
                    part_copy(d, u, m).wait_send()

            @pl.when((u < units) & (p > 0))
            def _():
                hid_copy(d, u).wait_send()


def solution(mesh):
    nf, nx, nr = mesh.shape["feat"], mesh.shape["tok"], mesh.shape["rep"]

    def shards(tokens, gate_weight, up_weight, down_weight, gate_mask, up_mask, down_mask):
        rows, feats = tokens.shape
        hidden = gate_weight.shape[1]
        width = 2 * BLOCK if hidden % (4 * BLOCK) == 0 else BLOCK
        chunks = hidden // width
        units = nx * ((chunks + 1) // 2)
        high = nr * rows
        bf16, f32 = jnp.bfloat16, jnp.float32
        dma = pltpu.SemaphoreType.DMA
        hbm, smem = pl.BlockSpec(memory_space=pl.ANY), pl.BlockSpec(memory_space=pltpu.SMEM)
        return pl.pallas_call(
            functools.partial(kernel, nf, nx, nr),
            out_shape=jax.ShapeDtypeStruct((rows, feats), bf16),
            in_specs=[hbm] * 4 + [smem] * 3,
            out_specs=pl.BlockSpec(memory_space=pltpu.VMEM),
            scratch_shapes=[
                pltpu.VMEM((nx * nr, rows, feats), bf16),
                pltpu.VMEM((nx, high, feats), bf16),
                pltpu.VMEM((chunks, feats, 2 * width), bf16),
                pltpu.VMEM((chunks, width, feats), bf16),
                pltpu.VMEM((2, 2, nr, rows, 2 * width), f32),
                pltpu.VMEM((2, units, nr, rows, 2 * width), bf16),
                pltpu.VMEM((2, units, nr, rows, 2 * width), bf16),
                pltpu.VMEM((2, units, high, width), bf16),
                pltpu.VMEM((nx, high, feats), f32),
                pltpu.VMEM((nx * nr, rows, feats), bf16),
                pltpu.VMEM((nx * nr, rows, feats), bf16),
                dma((nx * nr,)), dma((nx * nr,)), dma(()),
                dma((chunks,)), dma((chunks,)), dma((chunks,)),
                dma((2, units, nr)), dma((2, units, nr)), dma((2, units)), dma((2, units)),
                dma((nx * nr,)), dma((nx * nr,)),
            ],
            compiler_params=pltpu.CompilerParams(
                collective_id=0, has_side_effects=True, vmem_limit_bytes=63 * 1024 * 1024),
        )(tokens, gate_weight, up_weight, down_weight, gate_mask, up_mask, down_mask.T)

    return jax.shard_map(
        shards,
        mesh=mesh,
        in_specs=(
            P(("groups", "tok", "rep"), "feat"),
            P("feat", ("tok", "rep")),
            P("feat", ("tok", "rep")),
            P(("tok", "rep"), "feat"),
            P("feat", ("tok", "rep")),
            P("feat", ("tok", "rep")),
            P(("tok", "rep"), "feat"),
        ),
        out_specs=P(("groups", "tok", "rep"), "feat"),
        check_vma=False,
    )
```

```python
import functools

import jax
import jax.numpy as jnp
from jax import lax
from jax.experimental import pallas as pl
from jax.experimental.pallas import tpu as pltpu
from jax.sharding import PartitionSpec as P

BLOCK = 128
HOP = 3
BACK = 3
LEAD = 2
SLACK = 2
EARLY = 5
HEADS = 2
PAUSE = 2
MESH = pl.DeviceIdType.MESH


def kernel(nf, nx, nr, tokens, gate_w, up_w, down_w, gate_m, up_m, down_m, out,
           arrived, tok, wgu, wd, sums, part, taken, hid, acc, leaving, coming, shared, crossed,
           tok_send, tok_recv, own_sem, g_sem, u_sem, d_sem, part_send, part_recv,
           hid_send, hid_recv, out_send, out_recv, cross_send, cross_recv):
    z, x, r = lax.axis_index("feat"), lax.axis_index("tok"), lax.axis_index("rep")
    rows = arrived.shape[1]
    feats = tok.shape[2]
    chunks = wgu.shape[0]
    width = wd.shape[1]
    up_chunks, down_chunks = (chunks + 1) // 2, chunks // 2
    early = min(EARLY, down_chunks)
    peers = [(g, q) for g in range(nx) for q in range(nr)]

    def chip(g):
        return lax.rem(x + 1 + g, nx)

    barrier = pltpu.get_barrier_semaphore()
    for g in range(nx - 1):
        for q in range(nr):
            pl.semaphore_signal(barrier, inc=1, device_id={"tok": chip(g), "rep": q}, device_id_type=MESH)
    for step in range(1, nr):
        pl.semaphore_signal(barrier, inc=1, device_id={"rep": lax.rem(r + step, nr)}, device_id_type=MESH)

    @pl.when(z > 0)
    def _():
        pl.semaphore_signal(barrier, inc=1, device_id={"feat": z - 1}, device_id_type=MESH)

    @pl.when(z < nf - 1)
    def _():
        pl.semaphore_signal(barrier, inc=1, device_id={"feat": z + 1}, device_id_type=MESH)

    def gate_copy(j):
        cols = pl.ds(pl.multiple_of(j * width, width), width)
        return pltpu.make_async_copy(gate_w.at[:, cols], wgu.at[j, :, pl.ds(0, width)], g_sem.at[j])

    def up_copy(j):
        cols = pl.ds(pl.multiple_of(j * width, width), width)
        return pltpu.make_async_copy(up_w.at[:, cols], wgu.at[j, :, pl.ds(width, width)], u_sem.at[j])

    def down_copy(j):
        at = pl.ds(pl.multiple_of(j * width, width), width)
        return pltpu.make_async_copy(down_w.at[at, :], wd.at[j], d_sem.at[j])

    own_copy = pltpu.make_async_copy(tokens, arrived.at[(nx - 1) * nr + r], own_sem)
    own_copy.start()

    lead = min(LEAD, down_chunks)
    for c in range(lead):
        for e in range(2):
            j = jnp.where((z <= nf - 1 - z) == (e == 0), 0, up_chunks) + c
            gate_copy(j).start(priority=1)
            up_copy(j).start(priority=1)
    acc[...] = jnp.zeros_like(acc)

    def splat(scalar, shape):
        return jnp.full(shape, scalar.astype(jnp.float32)).astype(jnp.bfloat16)

    def product(left, j):
        total = None
        deep = 2 * BLOCK if feats % (2 * BLOCK) == 0 else BLOCK
        for lo in range(0, feats, deep):
            tall = []
            for b in range(lo // BLOCK, (lo + deep) // BLOCK):
                wide = []
                for n in range(2 * width // BLOCK):
                    mask = gate_m if n < width // BLOCK else up_m
                    keep = mask[b, j * (width // BLOCK) + n % (width // BLOCK)]
                    wide.append(wgu[j, b * BLOCK:(b + 1) * BLOCK, n * BLOCK:(n + 1) * BLOCK] * splat(keep, (BLOCK, BLOCK)))
                tall.append(jnp.concatenate(wide, axis=1))
            piece = jnp.dot(left[:, lo:lo + deep], jnp.concatenate(tall, axis=0), preferred_element_type=jnp.float32)
            total = piece if total is None else total + piece
        return total

    def ahead(d):
        return z + 1 - 2 * d

    def behind(d):
        return z - 1 + 2 * d

    def part_copy(d, u, m):
        return pltpu.make_async_remote_copy(
            src_ref=part.at[d, u, m], dst_ref=taken.at[d, u, m],
            send_sem=part_send.at[d, u, m], recv_sem=part_recv.at[d, u, m],
            device_id={"feat": ahead(d)}, device_id_type=MESH)

    heads = min(HEADS, down_chunks, early) if nr == 2 and nf > 1 else 0
    own_copy.wait()
    side = (z > 0).astype(jnp.int32)

    @pl.when((z == 0) | (z == nf - 1))
    def _():
        @pl.loop(0, heads)
        def _(c):
            j = side * up_chunks + c
            gate_copy(j).wait()
            up_copy(j).wait()
            part[side, c, 0] = product(arrived[(nx - 1) * nr + r], j).astype(jnp.bfloat16)

    ends = (z == 0).astype(jnp.int32) + (z == nf - 1).astype(jnp.int32)
    pl.semaphore_wait(barrier, nx * nr + 1 - ends)

    def near_copy(step):
        return pltpu.make_async_remote_copy(
            src_ref=tokens, dst_ref=arrived.at[(nx - 1) * nr + r],
            send_sem=tok_send.at[(nx - 1) * nr + step], recv_sem=tok_recv.at[(nx - 1) * nr + r],
            device_id={"rep": lax.rem(r + step, nr)}, device_id_type=MESH)

    def far_copy(g, q):
        slot = (nx - 2 - g) * nr + r
        return pltpu.make_async_remote_copy(
            src_ref=tokens, dst_ref=arrived.at[slot],
            send_sem=tok_send.at[g * nr + q], recv_sem=tok_recv.at[slot],
            device_id={"tok": chip(g), "rep": q}, device_id_type=MESH)

    def landed(slot):
        pltpu.make_async_remote_copy(
            src_ref=tokens, dst_ref=arrived.at[slot],
            send_sem=tok_send.at[0], recv_sem=tok_recv.at[slot],
            device_id={"rep": lax.rem(r + 1, nr)}, device_id_type=MESH).wait_recv()

    @pl.when((z == 0) | (z == nf - 1))
    def _():
        @pl.loop(0, heads)
        def _(c):
            part_copy(side, c, 0).start()

    for step in range(1, nr):
        near_copy(step).start()
    for g in range(nx - 1):
        for q in range(nr):
            far_copy(g, q).start()
    for step in range(1, nr):
        landed((nx - 1) * nr + lax.rem(r + step, nr))
    for q in range(nr):
        tok[nx - 1, q * rows:(q + 1) * rows, :] = arrived[(nx - 1) * nr + q]

    def place(d):
        p = jnp.where(d == 0, z, nf - 1 - z)
        count = up_chunks if up_chunks == down_chunks else jnp.where(d == 0, up_chunks, down_chunks)
        return p, count, nx * count

    def unit(u, d, count):
        mine = (u < early) | (u >= early + (nx - 1) * count)
        other = jnp.maximum(u - early, 0)
        group = jnp.where(mine, nx - 1, other // count)
        c = jnp.where(u < early, u, jnp.where(mine, u - (nx - 1) * count, other % count))
        first = (u < early) | ((u >= 2 * early) & (u < early + count))
        return group, d * up_chunks + c, first

    def hidden_unit(h, count):
        others = (nx - 1) * count
        c = h - others
        return jnp.where(c < 0, early + h, jnp.where(c < early, c, h))

    def hid_copy(d, u):
        return pltpu.make_async_remote_copy(
            src_ref=hid.at[d, u], dst_ref=hid.at[d, u],
            send_sem=hid_send.at[d, u], recv_sem=hid_recv.at[d, u],
            device_id={"feat": behind(d)}, device_id_type=MESH)

    others = (nx - 1) * up_chunks
    begin = HOP * (nf - 1) + max(nr * (early + others) - others, (nr - 1) * nx * up_chunks) + SLACK

    def multiply(k, d):
        p, count, units = place(d)
        t = k - HOP * p + nr
        u = t // nr

        @pl.when((t >= 0) & (u < units) & (t % nr == 0))
        def _():
            group, j, first = unit(u, d, count)

            @pl.when(u + lead < count)
            def _():
                gate_copy(d * up_chunks + u + lead).start(priority=1)
                up_copy(d * up_chunks + u + lead).start(priority=1)

            below = u - (count - lead if nx > 1 else 0)

            @pl.when((below >= 0) & (below < count))
            def _():
                down_copy(d * up_chunks + below).start(priority=1)

            @pl.when(first & ((p > 0) | (u >= heads)))
            def _():
                gate_copy(j).wait()
                up_copy(j).wait()

            total = product(tok[group], j)
            for m in range(nr):
                sums[d, u % 2, m] = total[m * rows:(m + 1) * rows, :]

    def reduce(k, d):
        p, count, units = place(d)
        t = k - HOP * p
        u, m = t // nr, t % nr
        if heads == 2:
            u, m = jnp.where(t < 4, t % 2, u), jnp.where(t < 4, t // 2, m)
        block = (r + m) % nr

        @pl.when((t >= jnp.where(p == 0, heads, 0)) & (u < units))
        def _():
            here = sums.at[d, u % 2, block]

            @pl.when(p > 0)
            def _():
                part_copy(d, u, m).wait_recv()
                here[...] += taken[d, u, m].astype(jnp.float32)

            @pl.when(p < nf - 1)
            def _():
                part[d, u, m] = here[...].astype(jnp.bfloat16)
                part_copy(d, u, m).start()

            for s in range(nr):
                @pl.when((p == nf - 1) & (block == s))
                def _():
                    gate, up = here[:, :width], here[:, width:]
                    hid[d, u, s * rows:(s + 1) * rows, :] = (gate / (1.0 + jnp.exp(-gate)) * up).astype(jnp.bfloat16)

    def spread(k, d):
        p, count, units = place(d)
        h = k - begin - BACK * (nf - 1 - p)

        @pl.when((h >= 0) & (h < units))
        def _():
            u = hidden_unit(h, count)
            group, j, _ = unit(u, d, count)

            @pl.when(p < nf - 1)
            def _():
                hid_copy(d, u).wait_recv()

            @pl.when(p > 0)
            def _():
                hid_copy(d, u).start()

            @pl.when(h < count)
            def _():
                down_copy(j).wait()

            for n in range(wd.shape[2] // BLOCK // 2):
                cols = slice(2 * n * BLOCK, 2 * (n + 1) * BLOCK)
                tall = []
                for b in range(width // BLOCK):
                    wide = []
                    for m in (2 * n, 2 * n + 1):
                        keep = down_m[m, j * (width // BLOCK) + b]
                        wide.append(wd[j, b * BLOCK:(b + 1) * BLOCK, m * BLOCK:(m + 1) * BLOCK] * splat(keep, (BLOCK, BLOCK)))
                    tall.append(jnp.concatenate(wide, axis=1))
                acc[group, :, cols] += jnp.dot(hid[d, u], jnp.concatenate(tall, axis=0),
                                               preferred_element_type=jnp.float32)

    def cross_copy(g, step):
        return pltpu.make_async_remote_copy(
            src_ref=shared.at[g, step], dst_ref=crossed.at[g, r],
            send_sem=cross_send.at[g, step], recv_sem=cross_recv.at[g, r],
            device_id={"rep": lax.rem(r + step, nr)}, device_id_type=MESH)

    def crossing(g, q):
        return pltpu.make_async_remote_copy(
            src_ref=shared.at[g, 0], dst_ref=crossed.at[g, q],
            send_sem=cross_send.at[g, 0], recv_sem=cross_recv.at[g, q],
            device_id={"rep": lax.rem(r + 1, nr)}, device_id_type=MESH)

    def out_copy(g):
        return pltpu.make_async_remote_copy(
            src_ref=leaving.at[g], dst_ref=coming.at[g],
            send_sem=out_send.at[g], recv_sem=out_recv.at[g],
            device_id={"tok": chip(g)}, device_id_type=MESH)

    def row_block(q):
        return pl.ds(pl.multiple_of(q * rows, 8), rows)

    def last_copy(step):
        return pltpu.make_async_remote_copy(
            src_ref=leaving.at[nx - 1 + step], dst_ref=coming.at[nx - 1 + r],
            send_sem=out_send.at[nx - 1 + step], recv_sem=out_recv.at[nx - 1 + r],
            device_id={"rep": lax.rem(r + step, nr)}, device_id_type=MESH)

    starts = HOP * jnp.minimum(z, nf - 1 - z) + nr * early - nr
    flip = (z > nf - 1 - z).astype(jnp.int32)

    @pl.loop(-nr, begin + BACK * (nf - 1) + nx * up_chunks)
    def _(k):
        @pl.loop(0, 2)
        def _(e):
            reduce(k, (e + flip) % 2)

        @pl.when(k == starts)
        def _():
            for g in range(nx - 1):
                for q in range(nr):
                    landed(g * nr + q)
                    tok[g, q * rows:(q + 1) * rows, :] = arrived[g * nr + q]

        @pl.loop(0, 2)
        def _(e):
            multiply(k, (e + flip) % 2)

        @pl.loop(0, 2)
        def _(e):
            spread(k, (e + flip) % 2)

        for g in range(nx - 1):
            ends = [begin + BACK * (nf - 1 - p) + (g + 1) * count - 1
                    for count, p in ((up_chunks, z), (down_chunks, nf - 1 - z))]

            @pl.when(k == jnp.maximum(*ends))
            def _():
                for step in range(1, nr):
                    shared[g, step] = acc[g, row_block(lax.rem(r + step, nr)), :].astype(jnp.bfloat16)
                    cross_copy(g, step).start()

            @pl.when(k == jnp.maximum(*ends) + PAUSE)
            def _():
                total = acc[g, row_block(r), :]
                for step in range(1, nr):
                    q = lax.rem(r + step, nr)
                    crossing(g, q).wait_recv()
                    total += crossed[g, q].astype(jnp.float32)
                leaving[g] = total.astype(jnp.bfloat16)
                out_copy(g).start()

    for step in range(1, nr):
        leaving[nx - 1 + step] = acc[nx - 1, row_block(lax.rem(r + step, nr)), :].astype(jnp.bfloat16)
        last_copy(step).start()
    final = acc[nx - 1, row_block(r), :]

    def summed(slot):
        pltpu.make_async_remote_copy(
            src_ref=leaving.at[0], dst_ref=coming.at[slot],
            send_sem=out_send.at[0], recv_sem=out_recv.at[slot],
            device_id={"rep": lax.rem(r + 1, nr)}, device_id_type=MESH).wait_recv()
        return coming[slot].astype(jnp.float32)

    for g in range(nx - 1):
        final += summed(nx - 2 - g)
    for step in range(1, nr):
        final += summed(nx - 1 + lax.rem(r + step, nr))
    out[...] = final.astype(out.dtype)

    for step in range(1, nr):
        near_copy(step).wait_send()
        last_copy(step).wait_send()
    for g in range(nx - 1):
        for q in range(nr):
            far_copy(g, q).wait_send()
        for step in range(1, nr):
            cross_copy(g, step).wait_send()
        out_copy(g).wait_send()

    @pl.loop(0, 2)
    def _(d):
        p, count, units = place(d)

        @pl.loop(0, nx * up_chunks)
        def _(u):
            @pl.when((u < units) & (p < nf - 1))
            def _():
                for m in range(nr):
                    part_copy(d, u, m).wait_send()

            @pl.when((u < units) & (p > 0))
            def _():
                hid_copy(d, u).wait_send()


def solution(mesh):
    nf, nx, nr = mesh.shape["feat"], mesh.shape["tok"], mesh.shape["rep"]

    def shards(tokens, gate_weight, up_weight, down_weight, gate_mask, up_mask, down_mask):
        rows, feats = tokens.shape
        hidden = gate_weight.shape[1]
        width = 2 * BLOCK if hidden % (4 * BLOCK) == 0 else BLOCK
        chunks = hidden // width
        units = nx * ((chunks + 1) // 2)
        high = nr * rows
        bf16, f32 = jnp.bfloat16, jnp.float32
        dma = pltpu.SemaphoreType.DMA
        hbm, smem = pl.BlockSpec(memory_space=pl.ANY), pl.BlockSpec(memory_space=pltpu.SMEM)
        return pl.pallas_call(
            functools.partial(kernel, nf, nx, nr),
            out_shape=pltpu.VMEM((rows, feats), bf16),
            in_specs=[hbm] * 4 + [smem] * 3,
            out_specs=pl.BlockSpec(memory_space=pltpu.VMEM),
            scratch_shapes=[
                pltpu.VMEM((nx * nr, rows, feats), bf16),
                pltpu.VMEM((nx, high, feats), bf16),
                pltpu.VMEM((chunks, feats, 2 * width), bf16),
                pltpu.VMEM((chunks, width, feats), bf16),
                pltpu.VMEM((2, 2, nr, rows, 2 * width), f32),
                pltpu.VMEM((2, units, nr, rows, 2 * width), bf16),
                pltpu.VMEM((2, units, nr, rows, 2 * width), bf16),
                pltpu.VMEM((2, units, high, width), bf16),
                pltpu.VMEM((nx, high, feats), f32),
                pltpu.VMEM((nx - 1 + nr, rows, feats), bf16),
                pltpu.VMEM((nx - 1 + nr, rows, feats), bf16),
                pltpu.VMEM((max(nx - 1, 1), nr, rows, feats), bf16),
                pltpu.VMEM((max(nx - 1, 1), nr, rows, feats), bf16),
                dma((nx * nr,)), dma((nx * nr,)), dma(()),
                dma((chunks,)), dma((chunks,)), dma((chunks,)),
                dma((2, units, nr)), dma((2, units, nr)), dma((2, units)), dma((2, units)),
                dma((nx - 1 + nr,)), dma((nx - 1 + nr,)),
                dma((max(nx - 1, 1), nr)), dma((max(nx - 1, 1), nr)),
            ],
            compiler_params=pltpu.CompilerParams(
                collective_id=0, has_side_effects=True, vmem_limit_bytes=63 * 1024 * 1024),
        )(tokens, gate_weight, up_weight, down_weight, gate_mask, up_mask, down_mask.T)

    return jax.shard_map(
        shards,
        mesh=mesh,
        in_specs=(
            P(("groups", "tok", "rep"), "feat"),
            P("feat", ("tok", "rep")),
            P("feat", ("tok", "rep")),
            P(("tok", "rep"), "feat"),
            P("feat", ("tok", "rep")),
            P("feat", ("tok", "rep")),
            P(("tok", "rep"), "feat"),
        ),
        out_specs=P(("groups", "tok", "rep"), "feat"),
        check_vma=False,
    )
```

```python
import functools

import jax
import jax.numpy as jnp
from jax import lax
from jax.experimental import pallas as pl
from jax.experimental.pallas import tpu as pltpu
from jax.sharding import PartitionSpec as P

BLOCK = 128
HOP = 3
BACK = 4
LEAD = 2
SLACK = 1
EARLY = 5
HEADS = 2
PAUSE = 2
TAIL = 512
MESH = pl.DeviceIdType.MESH


def kernel(nf, nx, nr, tokens, gate_w, up_w, down_w, gate_m, up_m, down_m, out,
           arrived, tok, wgu, wd, sums, part, taken, hid, acc, leaving, coming, shared, crossed, ending, ended,
           tok_send, tok_recv, own_sem, g_sem, u_sem, d_sem, part_send, part_recv,
           hid_send, hid_recv, out_send, out_recv, cross_send, cross_recv, end_send, end_recv):
    z, x, r = lax.axis_index("feat"), lax.axis_index("tok"), lax.axis_index("rep")
    rows = arrived.shape[1]
    feats = tok.shape[2]
    chunks = wgu.shape[0]
    width = wd.shape[1]
    up_chunks, down_chunks = (chunks + 1) // 2, chunks // 2
    early = min(EARLY, down_chunks)
    tail = TAIL if feats % TAIL == 0 else 2 * BLOCK
    peers = [(g, q) for g in range(nx) for q in range(nr)]

    def chip(g):
        return lax.rem(x + 1 + g, nx)

    barrier = pltpu.get_barrier_semaphore()
    for g in range(nx - 1):
        for q in range(nr):
            pl.semaphore_signal(barrier, inc=1, device_id={"tok": chip(g), "rep": q}, device_id_type=MESH)
    for step in range(1, nr):
        pl.semaphore_signal(barrier, inc=1, device_id={"rep": lax.rem(r + step, nr)}, device_id_type=MESH)

    @pl.when(z > 0)
    def _():
        pl.semaphore_signal(barrier, inc=1, device_id={"feat": z - 1}, device_id_type=MESH)

    @pl.when(z < nf - 1)
    def _():
        pl.semaphore_signal(barrier, inc=1, device_id={"feat": z + 1}, device_id_type=MESH)

    def gate_copy(j):
        cols = pl.ds(pl.multiple_of(j * width, width), width)
        return pltpu.make_async_copy(gate_w.at[:, cols], wgu.at[j, :, pl.ds(0, width)], g_sem.at[j])

    def up_copy(j):
        cols = pl.ds(pl.multiple_of(j * width, width), width)
        return pltpu.make_async_copy(up_w.at[:, cols], wgu.at[j, :, pl.ds(width, width)], u_sem.at[j])

    def down_copy(j):
        at = pl.ds(pl.multiple_of(j * width, width), width)
        return pltpu.make_async_copy(down_w.at[at, :], wd.at[j], d_sem.at[j])

    own_copy = pltpu.make_async_copy(tokens, arrived.at[(nx - 1) * nr + r], own_sem)
    own_copy.start()

    lead = min(LEAD, down_chunks)
    for c in range(lead):
        for e in range(2):
            near = jnp.minimum(z, nf - 1 - z)
            p = near if e == 0 else nf - 1 - near
            j = jnp.where((z <= nf - 1 - z) == (e == 0), 0, up_chunks) + c

            @pl.when(nr * c + HOP * p < nr * lead)
            def _():
                gate_copy(j).start(priority=1)
                up_copy(j).start(priority=1)

    acc[...] = jnp.zeros_like(acc)

    def splat(scalar, shape):
        return jnp.full(shape, scalar.astype(jnp.float32)).astype(jnp.bfloat16)

    def product(left, j):
        total = None
        deep = 2 * BLOCK if feats % (2 * BLOCK) == 0 else BLOCK
        for lo in range(0, feats, deep):
            tall = []
            for b in range(lo // BLOCK, (lo + deep) // BLOCK):
                wide = []
                for n in range(2 * width // BLOCK):
                    mask = gate_m if n < width // BLOCK else up_m
                    keep = mask[b, j * (width // BLOCK) + n % (width // BLOCK)]
                    wide.append(wgu[j, b * BLOCK:(b + 1) * BLOCK, n * BLOCK:(n + 1) * BLOCK] * splat(keep, (BLOCK, BLOCK)))
                tall.append(jnp.concatenate(wide, axis=1))
            piece = jnp.dot(left[:, lo:lo + deep], jnp.concatenate(tall, axis=0), preferred_element_type=jnp.float32)
            total = piece if total is None else total + piece
        return total

    def ahead(d):
        return z + 1 - 2 * d

    def behind(d):
        return z - 1 + 2 * d

    def part_copy(d, u, m):
        return pltpu.make_async_remote_copy(
            src_ref=part.at[d, u, m], dst_ref=taken.at[d, u, m],
            send_sem=part_send.at[d, u, m], recv_sem=part_recv.at[d, u, m],
            device_id={"feat": ahead(d)}, device_id_type=MESH)

    heads = min(HEADS, down_chunks, early) if nr == 2 and nf > 1 else 0
    own_copy.wait()
    side = (z > 0).astype(jnp.int32)

    def head(c):
        @pl.when((z == 0) | (z == nf - 1))
        def _():
            j = side * up_chunks + c
            gate_copy(j).wait()
            up_copy(j).wait()
            part[side, c, 0] = product(arrived[(nx - 1) * nr + r], j).astype(jnp.bfloat16)

    def send_head(c):
        @pl.when((z == 0) | (z == nf - 1))
        def _():
            part_copy(side, c, 0).start()

    if heads:
        head(0)

    ends = (z == 0).astype(jnp.int32) + (z == nf - 1).astype(jnp.int32)
    pl.semaphore_wait(barrier, nx * nr + 1 - ends)

    def near_copy(step):
        return pltpu.make_async_remote_copy(
            src_ref=tokens, dst_ref=arrived.at[(nx - 1) * nr + r],
            send_sem=tok_send.at[(nx - 1) * nr + step], recv_sem=tok_recv.at[(nx - 1) * nr + r],
            device_id={"rep": lax.rem(r + step, nr)}, device_id_type=MESH)

    def far_copy(g, q):
        slot = (nx - 2 - g) * nr + r
        return pltpu.make_async_remote_copy(
            src_ref=tokens, dst_ref=arrived.at[slot],
            send_sem=tok_send.at[g * nr + q], recv_sem=tok_recv.at[slot],
            device_id={"tok": chip(g), "rep": q}, device_id_type=MESH)

    def landed(slot):
        pltpu.make_async_remote_copy(
            src_ref=tokens, dst_ref=arrived.at[slot],
            send_sem=tok_send.at[0], recv_sem=tok_recv.at[slot],
            device_id={"rep": lax.rem(r + 1, nr)}, device_id_type=MESH).wait_recv()

    if heads:
        send_head(0)
    for step in range(1, nr):
        near_copy(step).start()
    for g in range(nx - 1):
        for q in range(nr):
            far_copy(g, q).start()

    if heads:
        @pl.loop(1, heads)
        def _(c):
            head(c)
            send_head(c)

    for step in range(1, nr):
        landed((nx - 1) * nr + lax.rem(r + step, nr))
    for q in range(nr):
        tok[nx - 1, q * rows:(q + 1) * rows, :] = arrived[(nx - 1) * nr + q]

    def place(d):
        p = jnp.where(d == 0, z, nf - 1 - z)
        count = up_chunks if up_chunks == down_chunks else jnp.where(d == 0, up_chunks, down_chunks)
        return p, count, nx * count

    def unit(u, d, count):
        mine = (u < early) | (u >= early + (nx - 1) * count)
        other = jnp.maximum(u - early, 0)
        group = jnp.where(mine, nx - 1, other // count)
        c = jnp.where(u < early, u, jnp.where(mine, u - (nx - 1) * count, other % count))
        first = (u < early) | ((u >= 2 * early) & (u < early + count))
        return group, d * up_chunks + c, first

    def hidden_unit(h, count):
        others = (nx - 1) * count
        c = h - others
        return jnp.where(c < 0, early + h, jnp.where(c < early, c, h))

    def hid_copy(d, u):
        return pltpu.make_async_remote_copy(
            src_ref=hid.at[d, u], dst_ref=hid.at[d, u],
            send_sem=hid_send.at[d, u], recv_sem=hid_recv.at[d, u],
            device_id={"feat": behind(d)}, device_id_type=MESH)

    others = (nx - 1) * up_chunks
    begin = HOP * (nf - 1) + max(nr * (early + others) - others, (nr - 1) * nx * up_chunks) + SLACK

    def prepare(k, d):
        p, count, units = place(d)
        t = k - HOP * p + nr + nr * lead
        c = t // nr

        @pl.when((t >= 0) & (c < count) & (t % nr == 0))
        def _():
            gate_copy(d * up_chunks + c).start(priority=1)
            up_copy(d * up_chunks + c).start(priority=1)

    def multiply(k, d):
        p, count, units = place(d)
        t = k - HOP * p + nr
        u = t // nr

        @pl.when((t >= 0) & (u < units) & (t % nr == 0))
        def _():
            group, j, first = unit(u, d, count)

            below = u - (count - lead if nx > 1 else 0)

            @pl.when((below >= 0) & (below < count))
            def _():
                down_copy(d * up_chunks + below).start(priority=1)

            @pl.when(first & ((p > 0) | (u >= heads)))
            def _():
                gate_copy(j).wait()
                up_copy(j).wait()

            total = product(tok[group], j)
            for m in range(nr):
                sums[d, u % 2, m] = total[m * rows:(m + 1) * rows, :]

    def reduce(k, d):
        p, count, units = place(d)
        t = k - HOP * p
        u, m = t // nr, t % nr
        if heads == 2:
            u, m = jnp.where(t < 4, t % 2, u), jnp.where(t < 4, t // 2, m)
        block = (r + m) % nr

        @pl.when((t >= jnp.where(p == 0, heads, 0)) & (u < units))
        def _():
            here = sums.at[d, u % 2, block]

            @pl.when(p > 0)
            def _():
                part_copy(d, u, m).wait_recv()
                here[...] += taken[d, u, m].astype(jnp.float32)

            @pl.when(p < nf - 1)
            def _():
                part[d, u, m] = here[...].astype(jnp.bfloat16)
                part_copy(d, u, m).start()

            for s in range(nr):
                @pl.when((p == nf - 1) & (block == s))
                def _():
                    gate, up = here[:, :width], here[:, width:]
                    hid[d, u, s * rows:(s + 1) * rows, :] = (gate / (1.0 + jnp.exp(-gate)) * up).astype(jnp.bfloat16)

    def lower(d, u, group, j, n):
        cols = slice(2 * n * BLOCK, 2 * (n + 1) * BLOCK)
        tall = []
        for b in range(width // BLOCK):
            wide = []
            for m in (2 * n, 2 * n + 1):
                keep = down_m[m, j * (width // BLOCK) + b]
                wide.append(wd[j, b * BLOCK:(b + 1) * BLOCK, m * BLOCK:(m + 1) * BLOCK] * splat(keep, (BLOCK, BLOCK)))
            tall.append(jnp.concatenate(wide, axis=1))
        acc[group, :, cols] += jnp.dot(hid[d, u], jnp.concatenate(tall, axis=0), preferred_element_type=jnp.float32)

    def pass_on(h, d):
        p, count, units = place(d)
        u = hidden_unit(h, count)
        group, j, _ = unit(u, d, count)

        @pl.when(p < nf - 1)
        def _():
            hid_copy(d, u).wait_recv()

        @pl.when(p > 0)
        def _():
            hid_copy(d, u).start()

        @pl.when(h < count)
        def _():
            down_copy(j).wait()

        return u, group, j

    flip = (z > nf - 1 - z).astype(jnp.int32)

    def spread(k, d):
        p, count, units = place(d)
        h = k - begin - BACK * (nf - 1 - p)

        @pl.when((h >= 0) & (h < units - (d == flip).astype(jnp.int32)))
        def _():
            u, group, j = pass_on(h, d)
            for n in range(feats // (2 * BLOCK)):
                lower(d, u, group, j, n)

    def cross_copy(g, step):
        return pltpu.make_async_remote_copy(
            src_ref=shared.at[g, step], dst_ref=crossed.at[g, r],
            send_sem=cross_send.at[g, step], recv_sem=cross_recv.at[g, r],
            device_id={"rep": lax.rem(r + step, nr)}, device_id_type=MESH)

    def crossing(g, q):
        return pltpu.make_async_remote_copy(
            src_ref=shared.at[g, 0], dst_ref=crossed.at[g, q],
            send_sem=cross_send.at[g, 0], recv_sem=cross_recv.at[g, q],
            device_id={"rep": lax.rem(r + 1, nr)}, device_id_type=MESH)

    def out_copy(g):
        return pltpu.make_async_remote_copy(
            src_ref=leaving.at[g], dst_ref=coming.at[g],
            send_sem=out_send.at[g], recv_sem=out_recv.at[g],
            device_id={"tok": chip(g)}, device_id_type=MESH)

    def row_block(q):
        return pl.ds(pl.multiple_of(q * rows, 8), rows)

    def last_copy(step, n):
        cols = pl.ds(n * tail, tail)
        return pltpu.make_async_remote_copy(
            src_ref=ending.at[step, :, cols], dst_ref=ended.at[r, :, cols],
            send_sem=end_send.at[step, n], recv_sem=end_recv.at[r, n],
            device_id={"rep": lax.rem(r + step, nr)}, device_id_type=MESH)

    def last_landed(q, n):
        cols = pl.ds(n * tail, tail)
        pltpu.make_async_remote_copy(
            src_ref=ending.at[0, :, cols], dst_ref=ended.at[q, :, cols],
            send_sem=end_send.at[0, n], recv_sem=end_recv.at[q, n],
            device_id={"rep": lax.rem(r + 1, nr)}, device_id_type=MESH).wait_recv()

    starts = HOP * jnp.minimum(z, nf - 1 - z) + nr * early - nr
    @pl.loop(-nr, begin + BACK * (nf - 1) + nx * up_chunks)
    def _(k):
        @pl.loop(0, 2)
        def _(e):
            reduce(k, (e + flip) % 2)

        @pl.when(k == starts)
        def _():
            for g in range(nx - 1):
                for q in range(nr):
                    landed(g * nr + q)
                    tok[g, q * rows:(q + 1) * rows, :] = arrived[g * nr + q]

        @pl.loop(0, 2)
        def _(e):
            prepare(k, (e + flip) % 2)
            multiply(k, (e + flip) % 2)

        @pl.loop(0, 2)
        def _(e):
            spread(k, (e + flip) % 2)

        for g in range(nx - 1):
            ends = [begin + BACK * (nf - 1 - p) + (g + 1) * count - 1
                    for count, p in ((up_chunks, z), (down_chunks, nf - 1 - z))]

            @pl.when(k == jnp.maximum(*ends))
            def _():
                for step in range(1, nr):
                    shared[g, step] = acc[g, row_block(lax.rem(r + step, nr)), :].astype(jnp.bfloat16)
                    cross_copy(g, step).start()

            @pl.when(k == jnp.maximum(*ends) + PAUSE)
            def _():
                total = acc[g, row_block(r), :]
                for step in range(1, nr):
                    q = lax.rem(r + step, nr)
                    crossing(g, q).wait_recv()
                    total += crossed[g, q].astype(jnp.float32)
                leaving[g] = total.astype(jnp.bfloat16)
                out_copy(g).start()

    _, _, last_units = place(flip)
    u, group, j = pass_on(last_units - 1, flip)
    for n in range(feats // tail):
        for b in range(tail // (2 * BLOCK)):
            lower(flip, u, nx - 1, j, n * (tail // (2 * BLOCK)) + b)
        cols = slice(n * tail, (n + 1) * tail)
        for step in range(1, nr):
            ending[step, :, cols] = acc[nx - 1, row_block(lax.rem(r + step, nr)), cols].astype(jnp.bfloat16)
            last_copy(step, n).start()

    own = row_block(r)
    for g in range(nx - 1):
        pltpu.make_async_remote_copy(
            src_ref=leaving.at[0], dst_ref=coming.at[g],
            send_sem=out_send.at[0], recv_sem=out_recv.at[g],
            device_id={"rep": lax.rem(r + 1, nr)}, device_id_type=MESH).wait_recv()
        acc[nx - 1, own, :] += coming[g].astype(jnp.float32)
    for n in range(feats // tail):
        cols = slice(n * tail, (n + 1) * tail)
        final = acc[nx - 1, own, cols]
        for step in range(1, nr):
            q = lax.rem(r + step, nr)
            last_landed(q, n)
            final += ended[q, :, cols].astype(jnp.float32)
        out[:, cols] = final.astype(out.dtype)

    for step in range(1, nr):
        near_copy(step).wait_send()
        for n in range(feats // tail):
            last_copy(step, n).wait_send()
    for g in range(nx - 1):
        for q in range(nr):
            far_copy(g, q).wait_send()
        for step in range(1, nr):
            cross_copy(g, step).wait_send()
        out_copy(g).wait_send()

    @pl.loop(0, 2)
    def _(d):
        p, count, units = place(d)

        @pl.loop(0, nx * up_chunks)
        def _(u):
            @pl.when((u < units) & (p < nf - 1))
            def _():
                for m in range(nr):
                    part_copy(d, u, m).wait_send()

            @pl.when((u < units) & (p > 0))
            def _():
                hid_copy(d, u).wait_send()


def solution(mesh):
    nf, nx, nr = mesh.shape["feat"], mesh.shape["tok"], mesh.shape["rep"]

    def shards(tokens, gate_weight, up_weight, down_weight, gate_mask, up_mask, down_mask):
        rows, feats = tokens.shape
        hidden = gate_weight.shape[1]
        width = 2 * BLOCK if hidden % (4 * BLOCK) == 0 else BLOCK
        chunks = hidden // width
        units = nx * ((chunks + 1) // 2)
        high = nr * rows
        pieces = feats // (TAIL if feats % TAIL == 0 else 2 * BLOCK)
        bf16, f32 = jnp.bfloat16, jnp.float32
        dma = pltpu.SemaphoreType.DMA
        hbm, smem = pl.BlockSpec(memory_space=pl.ANY), pl.BlockSpec(memory_space=pltpu.SMEM)
        return pl.pallas_call(
            functools.partial(kernel, nf, nx, nr),
            out_shape=pltpu.VMEM((rows, feats), bf16),
            in_specs=[hbm] * 4 + [smem] * 3,
            out_specs=pl.BlockSpec(memory_space=pltpu.VMEM),
            scratch_shapes=[
                pltpu.VMEM((nx * nr, rows, feats), bf16),
                pltpu.VMEM((nx, high, feats), bf16),
                pltpu.VMEM((chunks, feats, 2 * width), bf16),
                pltpu.VMEM((chunks, width, feats), bf16),
                pltpu.VMEM((2, 2, nr, rows, 2 * width), f32),
                pltpu.VMEM((2, units, nr, rows, 2 * width), bf16),
                pltpu.VMEM((2, units, nr, rows, 2 * width), bf16),
                pltpu.VMEM((2, units, high, width), bf16),
                pltpu.VMEM((nx, high, feats), f32),
                pltpu.VMEM((max(nx - 1, 1), rows, feats), bf16),
                pltpu.VMEM((max(nx - 1, 1), rows, feats), bf16),
                pltpu.VMEM((max(nx - 1, 1), nr, rows, feats), bf16),
                pltpu.VMEM((max(nx - 1, 1), nr, rows, feats), bf16),
                pltpu.VMEM((nr, rows, feats), bf16),
                pltpu.VMEM((nr, rows, feats), bf16),
                dma((nx * nr,)), dma((nx * nr,)), dma(()),
                dma((chunks,)), dma((chunks,)), dma((chunks,)),
                dma((2, units, nr)), dma((2, units, nr)), dma((2, units)), dma((2, units)),
                dma((max(nx - 1, 1),)), dma((max(nx - 1, 1),)),
                dma((max(nx - 1, 1), nr)), dma((max(nx - 1, 1), nr)),
                dma((nr, pieces)), dma((nr, pieces)),
            ],
            compiler_params=pltpu.CompilerParams(
                collective_id=0, has_side_effects=True, vmem_limit_bytes=63 * 1024 * 1024),
        )(tokens, gate_weight, up_weight, down_weight, gate_mask, up_mask, down_mask.T)

    return jax.shard_map(
        shards,
        mesh=mesh,
        in_specs=(
            P(("groups", "tok", "rep"), "feat"),
            P("feat", ("tok", "rep")),
            P("feat", ("tok", "rep")),
            P(("tok", "rep"), "feat"),
            P("feat", ("tok", "rep")),
            P("feat", ("tok", "rep")),
            P(("tok", "rep"), "feat"),
        ),
        out_specs=P(("groups", "tok", "rep"), "feat"),
        check_vma=False,
    )
```

```python
import functools

import jax
import jax.numpy as jnp
from jax import lax
from jax.experimental import pallas as pl
from jax.experimental.pallas import tpu as pltpu
from jax.sharding import PartitionSpec as P

BLOCK = 128
HOP = 3
BACK = 4
LEAD = 2
SLACK = 1
EARLY = 5
HEADS = 2
PAUSE = 2
TAIL = 512
MESH = pl.DeviceIdType.MESH


def kernel(nf, nx, nr, tokens, gate_w, up_w, down_w, gate_b, up_b, down_b, out,
           arrived, tok, wgu, wd, sums, part, taken, hid, acc, leaving, coming, shared, crossed, ending, ended, gate_m, up_m, down_m,
           tok_send, tok_recv, own_sem, g_sem, u_sem, d_sem, part_send, part_recv,
           hid_send, hid_recv, out_send, out_recv, cross_send, cross_recv, end_send, end_recv, mask_sem):
    z, x, r = lax.axis_index("feat"), lax.axis_index("tok"), lax.axis_index("rep")
    rows = arrived.shape[1]
    feats = tok.shape[2]
    chunks = wgu.shape[0]
    width = wd.shape[1]
    up_chunks, down_chunks = (chunks + 1) // 2, chunks // 2
    early = min(EARLY, down_chunks)
    tail = TAIL if feats % TAIL == 0 else 2 * BLOCK
    peers = [(g, q) for g in range(nx) for q in range(nr)]

    def chip(g):
        return lax.rem(x + 1 + g, nx)

    barrier = pltpu.get_barrier_semaphore()
    for g in range(nx - 1):
        for q in range(nr):
            pl.semaphore_signal(barrier, inc=1, device_id={"tok": chip(g), "rep": q}, device_id_type=MESH)
    for step in range(1, nr):
        pl.semaphore_signal(barrier, inc=1, device_id={"rep": lax.rem(r + step, nr)}, device_id_type=MESH)

    @pl.when(z > 0)
    def _():
        pl.semaphore_signal(barrier, inc=1, device_id={"feat": z - 1}, device_id_type=MESH)

    @pl.when(z < nf - 1)
    def _():
        pl.semaphore_signal(barrier, inc=1, device_id={"feat": z + 1}, device_id_type=MESH)

    def gate_copy(j):
        cols = pl.ds(pl.multiple_of(j * width, width), width)
        return pltpu.make_async_copy(gate_w.at[:, cols], wgu.at[j, :, pl.ds(0, width)], g_sem.at[j])

    def up_copy(j):
        cols = pl.ds(pl.multiple_of(j * width, width), width)
        return pltpu.make_async_copy(up_w.at[:, cols], wgu.at[j, :, pl.ds(width, width)], u_sem.at[j])

    def down_copy(j):
        at = pl.ds(pl.multiple_of(j * width, width), width)
        return pltpu.make_async_copy(down_w.at[at, :], wd.at[j], d_sem.at[j])

    own_copy = pltpu.make_async_copy(tokens, arrived.at[(nx - 1) * nr + r], own_sem)
    mask_copies = [pltpu.make_async_copy(src, dst, mask_sem.at[i])
                   for i, (src, dst) in enumerate(((gate_b, gate_m), (up_b, up_m), (down_b, down_m)))]
    for copy in mask_copies:
        copy.start()
    own_copy.start()

    lead = min(LEAD, down_chunks)
    for c in range(lead):
        for e in range(2):
            near = jnp.minimum(z, nf - 1 - z)
            p = near if e == 0 else nf - 1 - near
            j = jnp.where((z <= nf - 1 - z) == (e == 0), 0, up_chunks) + c

            @pl.when(nr * c + HOP * p < nr * lead)
            def _():
                gate_copy(j).start(priority=1)
                up_copy(j).start(priority=1)

    acc[...] = jnp.zeros_like(acc)

    def splat(scalar, shape):
        return jnp.full(shape, scalar.astype(jnp.float32)).astype(jnp.bfloat16)

    def product(left, j):
        total = None
        deep = 2 * BLOCK if feats % (2 * BLOCK) == 0 else BLOCK
        for lo in range(0, feats, deep):
            tall = []
            for b in range(lo // BLOCK, (lo + deep) // BLOCK):
                wide = []
                for n in range(2 * width // BLOCK):
                    mask = gate_m if n < width // BLOCK else up_m
                    keep = mask[b, j * (width // BLOCK) + n % (width // BLOCK)]
                    wide.append(wgu[j, b * BLOCK:(b + 1) * BLOCK, n * BLOCK:(n + 1) * BLOCK] * splat(keep, (BLOCK, BLOCK)))
                tall.append(jnp.concatenate(wide, axis=1))
            piece = jnp.dot(left[:, lo:lo + deep], jnp.concatenate(tall, axis=0), preferred_element_type=jnp.float32)
            total = piece if total is None else total + piece
        return total

    def ahead(d):
        return z + 1 - 2 * d

    def behind(d):
        return z - 1 + 2 * d

    def part_copy(d, u, m):
        return pltpu.make_async_remote_copy(
            src_ref=part.at[d, u, m], dst_ref=taken.at[d, u, m],
            send_sem=part_send.at[d, u, m], recv_sem=part_recv.at[d, u, m],
            device_id={"feat": ahead(d)}, device_id_type=MESH)

    heads = min(HEADS, down_chunks, early) if nr == 2 and nf > 1 else 0
    own_copy.wait()
    for copy in mask_copies:
        copy.wait()
    side = (z > 0).astype(jnp.int32)

    def head(c):
        @pl.when((z == 0) | (z == nf - 1))
        def _():
            j = side * up_chunks + c
            gate_copy(j).wait()
            up_copy(j).wait()
            part[side, c, 0] = product(arrived[(nx - 1) * nr + r], j).astype(jnp.bfloat16)

    def send_head(c):
        @pl.when((z == 0) | (z == nf - 1))
        def _():
            part_copy(side, c, 0).start()

    if heads:
        head(0)

    ends = (z == 0).astype(jnp.int32) + (z == nf - 1).astype(jnp.int32)
    pl.semaphore_wait(barrier, nx * nr + 1 - ends)

    def near_copy(step):
        return pltpu.make_async_remote_copy(
            src_ref=tokens, dst_ref=arrived.at[(nx - 1) * nr + r],
            send_sem=tok_send.at[(nx - 1) * nr + step], recv_sem=tok_recv.at[(nx - 1) * nr + r],
            device_id={"rep": lax.rem(r + step, nr)}, device_id_type=MESH)

    def far_copy(g, q):
        slot = (nx - 2 - g) * nr + r
        return pltpu.make_async_remote_copy(
            src_ref=tokens, dst_ref=arrived.at[slot],
            send_sem=tok_send.at[g * nr + q], recv_sem=tok_recv.at[slot],
            device_id={"tok": chip(g), "rep": q}, device_id_type=MESH)

    def landed(slot):
        pltpu.make_async_remote_copy(
            src_ref=tokens, dst_ref=arrived.at[slot],
            send_sem=tok_send.at[0], recv_sem=tok_recv.at[slot],
            device_id={"rep": lax.rem(r + 1, nr)}, device_id_type=MESH).wait_recv()

    if heads:
        send_head(0)
    for step in range(1, nr):
        near_copy(step).start()
    for g in range(nx - 1):
        for q in range(nr):
            far_copy(g, q).start()

    if heads:
        @pl.loop(1, heads)
        def _(c):
            head(c)
            send_head(c)

    for step in range(1, nr):
        landed((nx - 1) * nr + lax.rem(r + step, nr))
    for q in range(nr):
        tok[nx - 1, q * rows:(q + 1) * rows, :] = arrived[(nx - 1) * nr + q]

    def place(d):
        p = jnp.where(d == 0, z, nf - 1 - z)
        count = up_chunks if up_chunks == down_chunks else jnp.where(d == 0, up_chunks, down_chunks)
        return p, count, nx * count

    def unit(u, d, count):
        mine = (u < early) | (u >= early + (nx - 1) * count)
        other = jnp.maximum(u - early, 0)
        group = jnp.where(mine, nx - 1, other // count)
        c = jnp.where(u < early, u, jnp.where(mine, u - (nx - 1) * count, other % count))
        first = (u < early) | ((u >= 2 * early) & (u < early + count))
        return group, d * up_chunks + c, first

    def hidden_unit(h, count):
        others = (nx - 1) * count
        c = h - others
        return jnp.where(c < 0, early + h, jnp.where(c < early, c, h))

    def hid_copy(d, u):
        return pltpu.make_async_remote_copy(
            src_ref=hid.at[d, u], dst_ref=hid.at[d, u],
            send_sem=hid_send.at[d, u], recv_sem=hid_recv.at[d, u],
            device_id={"feat": behind(d)}, device_id_type=MESH)

    others = (nx - 1) * up_chunks
    begin = HOP * (nf - 1) + max(nr * (early + others) - others, (nr - 1) * nx * up_chunks) + SLACK

    def prepare(k, d):
        p, count, units = place(d)
        t = k - HOP * p + nr + nr * lead
        c = t // nr

        @pl.when((t >= 0) & (c < count) & (t % nr == 0))
        def _():
            gate_copy(d * up_chunks + c).start(priority=1)
            up_copy(d * up_chunks + c).start(priority=1)

    def multiply(k, d):
        p, count, units = place(d)
        t = k - HOP * p + nr
        u = t // nr

        @pl.when((t >= 0) & (u < units) & (t % nr == 0))
        def _():
            group, j, first = unit(u, d, count)

            below = u - (count - lead if nx > 1 else 0)

            @pl.when((below >= 0) & (below < count))
            def _():
                down_copy(d * up_chunks + below).start(priority=1)

            @pl.when(first & ((p > 0) | (u >= heads)))
            def _():
                gate_copy(j).wait()
                up_copy(j).wait()

            total = product(tok[group], j)
            for m in range(nr):
                sums[d, u % 2, m] = total[m * rows:(m + 1) * rows, :]

    def reduce(k, d):
        p, count, units = place(d)
        t = k - HOP * p
        u, m = t // nr, t % nr
        if heads == 2:
            u, m = jnp.where(t < 4, t % 2, u), jnp.where(t < 4, t // 2, m)
        block = (r + m) % nr

        @pl.when((t >= jnp.where(p == 0, heads, 0)) & (u < units))
        def _():
            here = sums.at[d, u % 2, block]

            @pl.when(p > 0)
            def _():
                part_copy(d, u, m).wait_recv()
                here[...] += taken[d, u, m].astype(jnp.float32)

            @pl.when(p < nf - 1)
            def _():
                part[d, u, m] = here[...].astype(jnp.bfloat16)
                part_copy(d, u, m).start()

            for s in range(nr):
                @pl.when((p == nf - 1) & (block == s))
                def _():
                    gate, up = here[:, :width], here[:, width:]
                    hid[d, u, s * rows:(s + 1) * rows, :] = (gate / (1.0 + jnp.exp(-gate)) * up).astype(jnp.bfloat16)

    def lower(d, u, group, j, n):
        cols = slice(2 * n * BLOCK, 2 * (n + 1) * BLOCK)
        tall = []
        for b in range(width // BLOCK):
            wide = []
            for m in (2 * n, 2 * n + 1):
                keep = down_m[m, j * (width // BLOCK) + b]
                wide.append(wd[j, b * BLOCK:(b + 1) * BLOCK, m * BLOCK:(m + 1) * BLOCK] * splat(keep, (BLOCK, BLOCK)))
            tall.append(jnp.concatenate(wide, axis=1))
        acc[group, :, cols] += jnp.dot(hid[d, u], jnp.concatenate(tall, axis=0), preferred_element_type=jnp.float32)

    def pass_on(h, d):
        p, count, units = place(d)
        u = hidden_unit(h, count)
        group, j, _ = unit(u, d, count)

        @pl.when(p < nf - 1)
        def _():
            hid_copy(d, u).wait_recv()

        @pl.when(p > 0)
        def _():
            hid_copy(d, u).start()

        @pl.when(h < count)
        def _():
            down_copy(j).wait()

        return u, group, j

    flip = (z > nf - 1 - z).astype(jnp.int32)

    def spread(k, d):
        p, count, units = place(d)
        h = k - begin - BACK * (nf - 1 - p)

        @pl.when((h >= 0) & (h < units - (d == flip).astype(jnp.int32)))
        def _():
            u, group, j = pass_on(h, d)
            for n in range(feats // (2 * BLOCK)):
                lower(d, u, group, j, n)

    def cross_copy(g, step):
        return pltpu.make_async_remote_copy(
            src_ref=shared.at[g, step], dst_ref=crossed.at[g, r],
            send_sem=cross_send.at[g, step], recv_sem=cross_recv.at[g, r],
            device_id={"rep": lax.rem(r + step, nr)}, device_id_type=MESH)

    def crossing(g, q):
        return pltpu.make_async_remote_copy(
            src_ref=shared.at[g, 0], dst_ref=crossed.at[g, q],
            send_sem=cross_send.at[g, 0], recv_sem=cross_recv.at[g, q],
            device_id={"rep": lax.rem(r + 1, nr)}, device_id_type=MESH)

    def out_copy(g):
        return pltpu.make_async_remote_copy(
            src_ref=leaving.at[g], dst_ref=coming.at[g],
            send_sem=out_send.at[g], recv_sem=out_recv.at[g],
            device_id={"tok": chip(g)}, device_id_type=MESH)

    def row_block(q):
        return pl.ds(pl.multiple_of(q * rows, 8), rows)

    def last_copy(step, n):
        cols = pl.ds(n * tail, tail)
        return pltpu.make_async_remote_copy(
            src_ref=ending.at[step, :, cols], dst_ref=ended.at[r, :, cols],
            send_sem=end_send.at[step, n], recv_sem=end_recv.at[r, n],
            device_id={"rep": lax.rem(r + step, nr)}, device_id_type=MESH)

    def last_landed(q, n):
        cols = pl.ds(n * tail, tail)
        pltpu.make_async_remote_copy(
            src_ref=ending.at[0, :, cols], dst_ref=ended.at[q, :, cols],
            send_sem=end_send.at[0, n], recv_sem=end_recv.at[q, n],
            device_id={"rep": lax.rem(r + 1, nr)}, device_id_type=MESH).wait_recv()

    starts = HOP * jnp.minimum(z, nf - 1 - z) + nr * early - nr
    @pl.loop(-nr, begin + BACK * (nf - 1) + nx * up_chunks)
    def _(k):
        @pl.loop(0, 2)
        def _(e):
            reduce(k, (e + flip) % 2)

        @pl.when(k == starts)
        def _():
            for g in range(nx - 1):
                for q in range(nr):
                    landed(g * nr + q)
                    tok[g, q * rows:(q + 1) * rows, :] = arrived[g * nr + q]

        @pl.loop(0, 2)
        def _(e):
            prepare(k, (e + flip) % 2)
            multiply(k, (e + flip) % 2)

        @pl.loop(0, 2)
        def _(e):
            spread(k, (e + flip) % 2)

        for g in range(nx - 1):
            ends = [begin + BACK * (nf - 1 - p) + (g + 1) * count - 1
                    for count, p in ((up_chunks, z), (down_chunks, nf - 1 - z))]

            @pl.when(k == jnp.maximum(*ends))
            def _():
                for step in range(1, nr):
                    shared[g, step] = acc[g, row_block(lax.rem(r + step, nr)), :].astype(jnp.bfloat16)
                    cross_copy(g, step).start()

            @pl.when(k == jnp.maximum(*ends) + PAUSE)
            def _():
                total = acc[g, row_block(r), :]
                for step in range(1, nr):
                    q = lax.rem(r + step, nr)
                    crossing(g, q).wait_recv()
                    total += crossed[g, q].astype(jnp.float32)
                leaving[g] = total.astype(jnp.bfloat16)
                out_copy(g).start()

    _, _, last_units = place(flip)
    u, group, j = pass_on(last_units - 1, flip)
    for n in range(feats // tail):
        for b in range(tail // (2 * BLOCK)):
            lower(flip, u, nx - 1, j, n * (tail // (2 * BLOCK)) + b)
        cols = slice(n * tail, (n + 1) * tail)
        for step in range(1, nr):
            ending[step, :, cols] = acc[nx - 1, row_block(lax.rem(r + step, nr)), cols].astype(jnp.bfloat16)
            last_copy(step, n).start()

    own = row_block(r)
    for g in range(nx - 1):
        pltpu.make_async_remote_copy(
            src_ref=leaving.at[0], dst_ref=coming.at[g],
            send_sem=out_send.at[0], recv_sem=out_recv.at[g],
            device_id={"rep": lax.rem(r + 1, nr)}, device_id_type=MESH).wait_recv()
        acc[nx - 1, own, :] += coming[g].astype(jnp.float32)
    for n in range(feats // tail):
        cols = slice(n * tail, (n + 1) * tail)
        final = acc[nx - 1, own, cols]
        for step in range(1, nr):
            q = lax.rem(r + step, nr)
            last_landed(q, n)
            final += ended[q, :, cols].astype(jnp.float32)
        out[:, cols] = final.astype(out.dtype)

    for step in range(1, nr):
        near_copy(step).wait_send()
        for n in range(feats // tail):
            last_copy(step, n).wait_send()
    for g in range(nx - 1):
        for q in range(nr):
            far_copy(g, q).wait_send()
        for step in range(1, nr):
            cross_copy(g, step).wait_send()
        out_copy(g).wait_send()

    @pl.loop(0, 2)
    def _(d):
        p, count, units = place(d)

        @pl.loop(0, nx * up_chunks)
        def _(u):
            @pl.when((u < units) & (p < nf - 1))
            def _():
                for m in range(nr):
                    part_copy(d, u, m).wait_send()

            @pl.when((u < units) & (p > 0))
            def _():
                hid_copy(d, u).wait_send()


def solution(mesh):
    nf, nx, nr = mesh.shape["feat"], mesh.shape["tok"], mesh.shape["rep"]

    def shards(tokens, gate_weight, up_weight, down_weight, gate_mask, up_mask, down_mask):
        rows, feats = tokens.shape
        hidden = gate_weight.shape[1]
        width = 2 * BLOCK if hidden % (4 * BLOCK) == 0 else BLOCK
        chunks = hidden // width
        units = nx * ((chunks + 1) // 2)
        high = nr * rows
        pieces = feats // (TAIL if feats % TAIL == 0 else 2 * BLOCK)
        bf16, f32 = jnp.bfloat16, jnp.float32
        dma = pltpu.SemaphoreType.DMA
        hbm = pl.BlockSpec(memory_space=pl.ANY)
        return pl.pallas_call(
            functools.partial(kernel, nf, nx, nr),
            out_shape=pltpu.VMEM((rows, feats), bf16),
            in_specs=[hbm] * 7,
            out_specs=pl.BlockSpec(memory_space=pltpu.VMEM),
            scratch_shapes=[
                pltpu.VMEM((nx * nr, rows, feats), bf16),
                pltpu.VMEM((nx, high, feats), bf16),
                pltpu.VMEM((chunks, feats, 2 * width), bf16),
                pltpu.VMEM((chunks, width, feats), bf16),
                pltpu.VMEM((2, 2, nr, rows, 2 * width), f32),
                pltpu.VMEM((2, units, nr, rows, 2 * width), bf16),
                pltpu.VMEM((2, units, nr, rows, 2 * width), bf16),
                pltpu.VMEM((2, units, high, width), bf16),
                pltpu.VMEM((nx, high, feats), f32),
                pltpu.VMEM((max(nx - 1, 1), rows, feats), bf16),
                pltpu.VMEM((max(nx - 1, 1), rows, feats), bf16),
                pltpu.VMEM((max(nx - 1, 1), nr, rows, feats), bf16),
                pltpu.VMEM((max(nx - 1, 1), nr, rows, feats), bf16),
                pltpu.VMEM((nr, rows, feats), bf16),
                pltpu.VMEM((nr, rows, feats), bf16),
                pltpu.SMEM(gate_mask.shape, jnp.int32), pltpu.SMEM(up_mask.shape, jnp.int32),
                pltpu.SMEM(down_mask.shape[::-1], jnp.int32),
                dma((nx * nr,)), dma((nx * nr,)), dma(()),
                dma((chunks,)), dma((chunks,)), dma((chunks,)),
                dma((2, units, nr)), dma((2, units, nr)), dma((2, units)), dma((2, units)),
                dma((max(nx - 1, 1),)), dma((max(nx - 1, 1),)),
                dma((max(nx - 1, 1), nr)), dma((max(nx - 1, 1), nr)),
                dma((nr, pieces)), dma((nr, pieces)), dma((3,)),
            ],
            compiler_params=pltpu.CompilerParams(
                collective_id=0, has_side_effects=True, vmem_limit_bytes=63 * 1024 * 1024),
        )(tokens, gate_weight, up_weight, down_weight, gate_mask, up_mask, down_mask.T)

    return jax.shard_map(
        shards,
        mesh=mesh,
        in_specs=(
            P(("groups", "tok", "rep"), "feat"),
            P("feat", ("tok", "rep")),
            P("feat", ("tok", "rep")),
            P(("tok", "rep"), "feat"),
            P("feat", ("tok", "rep")),
            P("feat", ("tok", "rep")),
            P(("tok", "rep"), "feat"),
        ),
        out_specs=P(("groups", "tok", "rep"), "feat"),
        check_vma=False,
    )
```

```python
import functools

import jax
import jax.numpy as jnp
from jax import lax
from jax.experimental import pallas as pl
from jax.experimental.pallas import tpu as pltpu
from jax.sharding import PartitionSpec as P

BLOCK = 128
HOP = 3
BACK = 4
LEAD = 2
SLACK = 1
EARLY = 5
HEADS = 2
PAUSE = 2
TAIL = 512
MESH = pl.DeviceIdType.MESH


def kernel(nf, nx, nr, tokens, gate_w, up_w, down_w, gate_b, up_b, down_b, out,
           arrived, tok, wgu, wd, sums, part, taken, hid, acc, leaving, coming, shared, crossed, ending, ended, gate_m, up_m, down_m,
           tok_send, tok_recv, own_sem, g_sem, u_sem, d_sem, part_send, part_recv,
           hid_send, hid_recv, out_send, out_recv, cross_send, cross_recv, end_send, end_recv, mask_sem):
    z, x, r = lax.axis_index("feat"), lax.axis_index("tok"), lax.axis_index("rep")
    rows = arrived.shape[1]
    feats = tok.shape[2]
    chunks = wgu.shape[0]
    width = wd.shape[1]
    up_chunks, down_chunks = (chunks + 1) // 2, chunks // 2
    early = min(EARLY, down_chunks)
    tail = TAIL if feats % TAIL == 0 else 2 * BLOCK
    peers = [(g, q) for g in range(nx) for q in range(nr)]

    def chip(g):
        return lax.rem(x + 1 + g, nx)

    barrier = pltpu.get_barrier_semaphore()
    for g in range(nx - 1):
        for q in range(nr):
            pl.semaphore_signal(barrier, inc=1, device_id={"tok": chip(g), "rep": q}, device_id_type=MESH)
    for step in range(1, nr):
        pl.semaphore_signal(barrier, inc=1, device_id={"rep": lax.rem(r + step, nr)}, device_id_type=MESH)

    @pl.when(z > 0)
    def _():
        pl.semaphore_signal(barrier, inc=1, device_id={"feat": z - 1}, device_id_type=MESH)

    @pl.when(z < nf - 1)
    def _():
        pl.semaphore_signal(barrier, inc=1, device_id={"feat": z + 1}, device_id_type=MESH)

    def gate_copy(j):
        cols = pl.ds(pl.multiple_of(j * width, width), width)
        return pltpu.make_async_copy(gate_w.at[:, cols], wgu.at[j, :, pl.ds(0, width)], g_sem.at[j])

    def up_copy(j):
        cols = pl.ds(pl.multiple_of(j * width, width), width)
        return pltpu.make_async_copy(up_w.at[:, cols], wgu.at[j, :, pl.ds(width, width)], u_sem.at[j])

    def down_copy(j):
        at = pl.ds(pl.multiple_of(j * width, width), width)
        return pltpu.make_async_copy(down_w.at[at, :], wd.at[j], d_sem.at[j])

    own_copy = pltpu.make_async_copy(tokens, arrived.at[(nx - 1) * nr + r], own_sem)
    mask_copies = [pltpu.make_async_copy(src, dst, mask_sem.at[i])
                   for i, (src, dst) in enumerate(((gate_b, gate_m), (up_b, up_m), (down_b, down_m)))]
    for copy in mask_copies:
        copy.start()
    own_copy.start()

    lead = min(LEAD, down_chunks)
    for c in range(lead):
        for e in range(2):
            near = jnp.minimum(z, nf - 1 - z)
            p = near if e == 0 else nf - 1 - near
            j = jnp.where((z <= nf - 1 - z) == (e == 0), 0, up_chunks) + c

            @pl.when(nr * c + HOP * p < nr * lead)
            def _():
                gate_copy(j).start(priority=1)
                up_copy(j).start(priority=1)

    acc[...] = jnp.zeros_like(acc)

    def splat(scalar, shape):
        return jnp.full(shape, scalar.astype(jnp.float32)).astype(jnp.bfloat16)

    def product(left, j):
        total = None
        deep = 2 * BLOCK if feats % (2 * BLOCK) == 0 else BLOCK
        for lo in range(0, feats, deep):
            tall = []
            for b in range(lo // BLOCK, (lo + deep) // BLOCK):
                wide = []
                for n in range(2 * width // BLOCK):
                    mask = gate_m if n < width // BLOCK else up_m
                    keep = mask[b, j * (width // BLOCK) + n % (width // BLOCK)]
                    wide.append(wgu[j, b * BLOCK:(b + 1) * BLOCK, n * BLOCK:(n + 1) * BLOCK] * splat(keep, (BLOCK, BLOCK)))
                tall.append(jnp.concatenate(wide, axis=1))
            piece = jnp.dot(left[:, lo:lo + deep], jnp.concatenate(tall, axis=0), preferred_element_type=jnp.float32)
            total = piece if total is None else total + piece
        return total

    def ahead(d):
        return z + 1 - 2 * d

    def behind(d):
        return z - 1 + 2 * d

    def part_copy(d, u, m):
        return pltpu.make_async_remote_copy(
            src_ref=part.at[d, u, m], dst_ref=taken.at[d, u, m],
            send_sem=part_send.at[d, u, m], recv_sem=part_recv.at[d, u, m],
            device_id={"feat": ahead(d)}, device_id_type=MESH)

    heads = min(HEADS, down_chunks, early) if nr == 2 and nf > 1 else 0
    own_copy.wait()
    for copy in mask_copies:
        copy.wait()
    side = (z > 0).astype(jnp.int32)

    def head(c):
        @pl.when((z == 0) | (z == nf - 1))
        def _():
            j = side * up_chunks + c
            gate_copy(j).wait()
            up_copy(j).wait()
            part[side, c, 0] = product(arrived[(nx - 1) * nr + r], j).astype(jnp.bfloat16)

    def send_head(c):
        @pl.when((z == 0) | (z == nf - 1))
        def _():
            part_copy(side, c, 0).start()

    if heads:
        head(0)

    ends = (z == 0).astype(jnp.int32) + (z == nf - 1).astype(jnp.int32)
    pl.semaphore_wait(barrier, nx * nr + 1 - ends)

    def near_copy(step):
        return pltpu.make_async_remote_copy(
            src_ref=tokens, dst_ref=arrived.at[(nx - 1) * nr + r],
            send_sem=tok_send.at[(nx - 1) * nr + step], recv_sem=tok_recv.at[(nx - 1) * nr + r],
            device_id={"rep": lax.rem(r + step, nr)}, device_id_type=MESH)

    def far_copy(g, q):
        slot = (nx - 2 - g) * nr + r
        return pltpu.make_async_remote_copy(
            src_ref=tokens, dst_ref=arrived.at[slot],
            send_sem=tok_send.at[g * nr + q], recv_sem=tok_recv.at[slot],
            device_id={"tok": chip(g), "rep": q}, device_id_type=MESH)

    def landed(slot):
        pltpu.make_async_remote_copy(
            src_ref=tokens, dst_ref=arrived.at[slot],
            send_sem=tok_send.at[0], recv_sem=tok_recv.at[slot],
            device_id={"rep": lax.rem(r + 1, nr)}, device_id_type=MESH).wait_recv()

    if heads:
        send_head(0)
    for step in range(1, nr):
        near_copy(step).start()
    for g in range(nx - 1):
        for q in range(nr):
            far_copy(g, q).start()

    if heads:
        @pl.loop(1, heads)
        def _(c):
            head(c)
            send_head(c)

    for step in range(1, nr):
        landed((nx - 1) * nr + lax.rem(r + step, nr))
    for q in range(nr):
        tok[nx - 1, q * rows:(q + 1) * rows, :] = arrived[(nx - 1) * nr + q]

    def place(d):
        p = jnp.where(d == 0, z, nf - 1 - z)
        count = up_chunks if up_chunks == down_chunks else jnp.where(d == 0, up_chunks, down_chunks)
        return p, count, nx * count

    def unit(u, d, count):
        mine = (u < early) | (u >= early + (nx - 1) * count)
        other = jnp.maximum(u - early, 0)
        group = jnp.where(mine, nx - 1, other // count)
        c = jnp.where(u < early, u, jnp.where(mine, u - (nx - 1) * count, other % count))
        first = (u < early) | ((u >= 2 * early) & (u < early + count))
        return group, d * up_chunks + c, first

    def hidden_unit(h, count):
        others = (nx - 1) * count
        c = h - others
        return jnp.where(c < 0, early + h, jnp.where(c < early, c, h))

    def hid_copy(d, u):
        return pltpu.make_async_remote_copy(
            src_ref=hid.at[d, u], dst_ref=hid.at[d, u],
            send_sem=hid_send.at[d, u], recv_sem=hid_recv.at[d, u],
            device_id={"feat": behind(d)}, device_id_type=MESH)

    others = (nx - 1) * up_chunks
    begin = HOP * (nf - 1) + max(nr * (early + others) - others, (nr - 1) * nx * up_chunks) + SLACK

    def prepare(k, d):
        p, count, units = place(d)
        t = k - HOP * p + nr + nr * lead
        c = t // nr

        @pl.when((t >= 0) & (c < count) & (t % nr == 0))
        def _():
            gate_copy(d * up_chunks + c).start(priority=1)
            up_copy(d * up_chunks + c).start(priority=1)

    def multiply(k, d):
        p, count, units = place(d)
        t = k - HOP * p + nr
        u = t // nr

        @pl.when((t >= 0) & (u < units) & (t % nr == 0))
        def _():
            group, j, first = unit(u, d, count)

            below = u - (count - lead if nx > 1 else 0)

            @pl.when((below >= 0) & (below < count))
            def _():
                down_copy(d * up_chunks + below).start(priority=1)

            @pl.when(first & ((p > 0) | (u >= heads)))
            def _():
                gate_copy(j).wait()
                up_copy(j).wait()

            total = product(tok[group], j)
            for m in range(nr):
                sums[d, u % 2, m] = total[m * rows:(m + 1) * rows, :]

    def reduce(k, d):
        p, count, units = place(d)
        t = k - HOP * p
        u, m = t // nr, t % nr
        if heads == 2:
            u, m = jnp.where(t < 4, t % 2, u), jnp.where(t < 4, t // 2, m)
        block = (r + m) % nr

        @pl.when((t >= jnp.where(p == 0, heads, 0)) & (u < units))
        def _():
            here = sums.at[d, u % 2, block]

            @pl.when(p > 0)
            def _():
                part_copy(d, u, m).wait_recv()
                here[...] += taken[d, u, m].astype(jnp.float32)

            @pl.when(p < nf - 1)
            def _():
                part[d, u, m] = here[...].astype(jnp.bfloat16)
                part_copy(d, u, m).start()

            for s in range(nr):
                @pl.when((p == nf - 1) & (block == s))
                def _():
                    gate, up = here[:, :width], here[:, width:]
                    hid[d, u, s * rows:(s + 1) * rows, :] = (gate / (1.0 + jnp.exp(-gate)) * up).astype(jnp.bfloat16)

    def lower(d, u, group, j, n):
        cols = slice(2 * n * BLOCK, 2 * (n + 1) * BLOCK)
        tall = []
        for b in range(width // BLOCK):
            wide = []
            for m in (2 * n, 2 * n + 1):
                keep = down_m[m, j * (width // BLOCK) + b]
                wide.append(wd[j, b * BLOCK:(b + 1) * BLOCK, m * BLOCK:(m + 1) * BLOCK] * splat(keep, (BLOCK, BLOCK)))
            tall.append(jnp.concatenate(wide, axis=1))
        acc[group, :, cols] += jnp.dot(hid[d, u], jnp.concatenate(tall, axis=0), preferred_element_type=jnp.float32)

    def pass_on(h, d):
        p, count, units = place(d)
        u = hidden_unit(h, count)
        group, j, _ = unit(u, d, count)

        @pl.when(p < nf - 1)
        def _():
            hid_copy(d, u).wait_recv()

        @pl.when(p > 0)
        def _():
            hid_copy(d, u).start()

        @pl.when(h < count)
        def _():
            down_copy(j).wait()

        return u, group, j

    flip = (z > nf - 1 - z).astype(jnp.int32)

    def spread(k, d):
        p, count, units = place(d)
        h = k - begin - BACK * (nf - 1 - p)

        @pl.when((h >= 0) & (h < units - (d == flip).astype(jnp.int32)))
        def _():
            u, group, j = pass_on(h, d)
            for n in range(feats // (2 * BLOCK)):
                lower(d, u, group, j, n)

    def cross_copy(g, step):
        return pltpu.make_async_remote_copy(
            src_ref=shared.at[g, step], dst_ref=crossed.at[g, r],
            send_sem=cross_send.at[g, step], recv_sem=cross_recv.at[g, r],
            device_id={"rep": lax.rem(r + step, nr)}, device_id_type=MESH)

    def crossing(g, q):
        return pltpu.make_async_remote_copy(
            src_ref=shared.at[g, 0], dst_ref=crossed.at[g, q],
            send_sem=cross_send.at[g, 0], recv_sem=cross_recv.at[g, q],
            device_id={"rep": lax.rem(r + 1, nr)}, device_id_type=MESH)

    def out_copy(g):
        return pltpu.make_async_remote_copy(
            src_ref=leaving.at[g], dst_ref=coming.at[g],
            send_sem=out_send.at[g], recv_sem=out_recv.at[g],
            device_id={"tok": chip(g)}, device_id_type=MESH)

    def row_block(q):
        return pl.ds(pl.multiple_of(q * rows, 8), rows)

    def last_copy(step, n):
        cols = pl.ds(n * tail, tail)
        return pltpu.make_async_remote_copy(
            src_ref=ending.at[step, :, cols], dst_ref=ended.at[r, :, cols],
            send_sem=end_send.at[step, n], recv_sem=end_recv.at[r, n],
            device_id={"rep": lax.rem(r + step, nr)}, device_id_type=MESH)

    def last_landed(q, n):
        cols = pl.ds(n * tail, tail)
        pltpu.make_async_remote_copy(
            src_ref=ending.at[0, :, cols], dst_ref=ended.at[q, :, cols],
            send_sem=end_send.at[0, n], recv_sem=end_recv.at[q, n],
            device_id={"rep": lax.rem(r + 1, nr)}, device_id_type=MESH).wait_recv()

    starts = HOP * jnp.minimum(z, nf - 1 - z) + nr * early - nr
    @pl.loop(-nr, begin + BACK * (nf - 1) + nx * up_chunks)
    def _(k):
        @pl.loop(0, 2)
        def _(e):
            reduce(k, (e + flip) % 2)

        @pl.when(k == starts)
        def _():
            for g in range(nx - 1):
                for q in range(nr):
                    landed(g * nr + q)
                    tok[g, q * rows:(q + 1) * rows, :] = arrived[g * nr + q]

        @pl.loop(0, 2)
        def _(e):
            prepare(k, (e + flip) % 2)
            multiply(k, (e + flip) % 2)

        @pl.loop(0, 2)
        def _(e):
            spread(k, (e + flip) % 2)

        for g in range(nx - 1):
            ends = [begin + BACK * (nf - 1 - p) + (g + 1) * count - 1
                    for count, p in ((up_chunks, z), (down_chunks, nf - 1 - z))]

            @pl.when(k == jnp.maximum(*ends))
            def _():
                for step in range(1, nr):
                    shared[g, step] = acc[g, row_block(lax.rem(r + step, nr)), :].astype(jnp.bfloat16)
                    cross_copy(g, step).start()

            @pl.when(k == jnp.maximum(*ends) + PAUSE)
            def _():
                total = acc[g, row_block(r), :]
                for step in range(1, nr):
                    q = lax.rem(r + step, nr)
                    crossing(g, q).wait_recv()
                    total += crossed[g, q].astype(jnp.float32)
                leaving[g] = total.astype(jnp.bfloat16)
                out_copy(g).start()

    _, _, last_units = place(flip)
    u, group, j = pass_on(last_units - 1, flip)
    for n in range(feats // tail):
        for b in range(tail // (2 * BLOCK)):
            lower(flip, u, nx - 1, j, n * (tail // (2 * BLOCK)) + b)
        cols = slice(n * tail, (n + 1) * tail)
        for step in range(1, nr):
            ending[step, :, cols] = acc[nx - 1, row_block(lax.rem(r + step, nr)), cols].astype(jnp.bfloat16)
            last_copy(step, n).start()

    for step in range(1, nr):
        near_copy(step).wait_send()
    for g in range(nx - 1):
        for q in range(nr):
            far_copy(g, q).wait_send()
        for step in range(1, nr):
            cross_copy(g, step).wait_send()
        out_copy(g).wait_send()

    @pl.loop(0, 2)
    def _(d):
        p, count, units = place(d)

        @pl.loop(0, nx * up_chunks)
        def _(u):
            @pl.when((u < units) & (p < nf - 1))
            def _():
                for m in range(nr):
                    part_copy(d, u, m).wait_send()

            @pl.when((u < units) & (p > 0))
            def _():
                hid_copy(d, u).wait_send()

    own = row_block(r)
    for g in range(nx - 1):
        pltpu.make_async_remote_copy(
            src_ref=leaving.at[0], dst_ref=coming.at[g],
            send_sem=out_send.at[0], recv_sem=out_recv.at[g],
            device_id={"rep": lax.rem(r + 1, nr)}, device_id_type=MESH).wait_recv()
        acc[nx - 1, own, :] += coming[g].astype(jnp.float32)
    for n in range(feats // tail):
        cols = slice(n * tail, (n + 1) * tail)
        final = acc[nx - 1, own, cols]
        for step in range(1, nr):
            q = lax.rem(r + step, nr)
            last_landed(q, n)
            final += ended[q, :, cols].astype(jnp.float32)
        out[:, cols] = final.astype(out.dtype)

    for step in range(1, nr):
        for n in range(feats // tail):
            last_copy(step, n).wait_send()


def solution(mesh):
    nf, nx, nr = mesh.shape["feat"], mesh.shape["tok"], mesh.shape["rep"]

    def shards(tokens, gate_weight, up_weight, down_weight, gate_mask, up_mask, down_mask):
        rows, feats = tokens.shape
        hidden = gate_weight.shape[1]
        width = 2 * BLOCK if hidden % (4 * BLOCK) == 0 else BLOCK
        chunks = hidden // width
        units = nx * ((chunks + 1) // 2)
        high = nr * rows
        pieces = feats // (TAIL if feats % TAIL == 0 else 2 * BLOCK)
        bf16, f32 = jnp.bfloat16, jnp.float32
        dma = pltpu.SemaphoreType.DMA
        hbm = pl.BlockSpec(memory_space=pl.ANY)
        return pl.pallas_call(
            functools.partial(kernel, nf, nx, nr),
            out_shape=pltpu.VMEM((rows, feats), bf16),
            in_specs=[hbm] * 7,
            out_specs=pl.BlockSpec(memory_space=pltpu.VMEM),
            scratch_shapes=[
                pltpu.VMEM((nx * nr, rows, feats), bf16),
                pltpu.VMEM((nx, high, feats), bf16),
                pltpu.VMEM((chunks, feats, 2 * width), bf16),
                pltpu.VMEM((chunks, width, feats), bf16),
                pltpu.VMEM((2, 2, nr, rows, 2 * width), f32),
                pltpu.VMEM((2, units, nr, rows, 2 * width), bf16),
                pltpu.VMEM((2, units, nr, rows, 2 * width), bf16),
                pltpu.VMEM((2, units, high, width), bf16),
                pltpu.VMEM((nx, high, feats), f32),
                pltpu.VMEM((max(nx - 1, 1), rows, feats), bf16),
                pltpu.VMEM((max(nx - 1, 1), rows, feats), bf16),
                pltpu.VMEM((max(nx - 1, 1), nr, rows, feats), bf16),
                pltpu.VMEM((max(nx - 1, 1), nr, rows, feats), bf16),
                pltpu.VMEM((nr, rows, feats), bf16),
                pltpu.VMEM((nr, rows, feats), bf16),
                pltpu.SMEM(gate_mask.shape, jnp.int32), pltpu.SMEM(up_mask.shape, jnp.int32),
                pltpu.SMEM(down_mask.shape[::-1], jnp.int32),
                dma((nx * nr,)), dma((nx * nr,)), dma(()),
                dma((chunks,)), dma((chunks,)), dma((chunks,)),
                dma((2, units, nr)), dma((2, units, nr)), dma((2, units)), dma((2, units)),
                dma((max(nx - 1, 1),)), dma((max(nx - 1, 1),)),
                dma((max(nx - 1, 1), nr)), dma((max(nx - 1, 1), nr)),
                dma((nr, pieces)), dma((nr, pieces)), dma((3,)),
            ],
            compiler_params=pltpu.CompilerParams(
                collective_id=0, has_side_effects=True, vmem_limit_bytes=63 * 1024 * 1024),
        )(tokens, gate_weight, up_weight, down_weight, gate_mask, up_mask, down_mask.T)

    return jax.shard_map(
        shards,
        mesh=mesh,
        in_specs=(
            P(("groups", "tok", "rep"), "feat"),
            P("feat", ("tok", "rep")),
            P("feat", ("tok", "rep")),
            P(("tok", "rep"), "feat"),
            P("feat", ("tok", "rep")),
            P("feat", ("tok", "rep")),
            P(("tok", "rep"), "feat"),
        ),
        out_specs=P(("groups", "tok", "rep"), "feat"),
        check_vma=False,
    )
```

```python
import functools

import jax
import jax.numpy as jnp
from jax import lax
from jax.experimental import pallas as pl
from jax.experimental.pallas import tpu as pltpu
from jax.sharding import PartitionSpec as P

BLOCK = 128
HOP = 3
BACK = 4
LEAD = 2
SLACK = 1
EARLY = 5
HEADS = 2
PAUSE = 2
TAIL = 512
MESH = pl.DeviceIdType.MESH


def kernel(nf, nx, nr, tokens, gate_w, up_w, down_w, gate_b, up_b, down_b, out,
           arrived, tok, wgu, wd, sums, part, taken, hid, acc, leaving, coming, shared, crossed, ending, ended, gate_m, up_m, down_m,
           tok_send, tok_recv, own_sem, g_sem, u_sem, d_sem, part_send, part_recv,
           hid_send, hid_recv, out_send, out_recv, cross_send, cross_recv, end_send, end_recv, mask_sem):
    z, x, r = lax.axis_index("feat"), lax.axis_index("tok"), lax.axis_index("rep")
    rows = arrived.shape[1]
    feats = tok.shape[2]
    chunks = wgu.shape[0]
    width = wd.shape[1]
    up_chunks, down_chunks = (chunks + 1) // 2, chunks // 2
    early = min(EARLY, down_chunks)
    tail = TAIL if feats % TAIL == 0 else 2 * BLOCK
    peers = [(g, q) for g in range(nx) for q in range(nr)]

    def chip(g):
        return lax.rem(x + 1 + g, nx)

    barrier = pltpu.get_barrier_semaphore()
    for g in range(nx - 1):
        for q in range(nr):
            pl.semaphore_signal(barrier, inc=1, device_id={"tok": chip(g), "rep": q}, device_id_type=MESH)
    for step in range(1, nr):
        pl.semaphore_signal(barrier, inc=1, device_id={"rep": lax.rem(r + step, nr)}, device_id_type=MESH)

    @pl.when(z > 0)
    def _():
        pl.semaphore_signal(barrier, inc=1, device_id={"feat": z - 1}, device_id_type=MESH)

    @pl.when(z < nf - 1)
    def _():
        pl.semaphore_signal(barrier, inc=1, device_id={"feat": z + 1}, device_id_type=MESH)

    def gate_copy(j):
        cols = pl.ds(pl.multiple_of(j * width, width), width)
        return pltpu.make_async_copy(gate_w.at[:, cols], wgu.at[j, :, pl.ds(0, width)], g_sem.at[j])

    def up_copy(j):
        cols = pl.ds(pl.multiple_of(j * width, width), width)
        return pltpu.make_async_copy(up_w.at[:, cols], wgu.at[j, :, pl.ds(width, width)], u_sem.at[j])

    def down_copy(j):
        at = pl.ds(pl.multiple_of(j * width, width), width)
        return pltpu.make_async_copy(down_w.at[at, :], wd.at[j], d_sem.at[j])

    own_copy = pltpu.make_async_copy(tokens, arrived.at[(nx - 1) * nr + r], own_sem)
    mask_copies = [pltpu.make_async_copy(src, dst, mask_sem.at[i])
                   for i, (src, dst) in enumerate(((gate_b, gate_m), (up_b, up_m), (down_b, down_m)))]
    for copy in mask_copies:
        copy.start()
    own_copy.start()

    lead = min(LEAD, down_chunks)
    for c in range(lead):
        for e in range(2):
            near = jnp.minimum(z, nf - 1 - z)
            p = near if e == 0 else nf - 1 - near
            j = jnp.where((z <= nf - 1 - z) == (e == 0), 0, up_chunks) + c

            @pl.when(nr * c + HOP * p < nr * lead)
            def _():
                gate_copy(j).start(priority=1)
                up_copy(j).start(priority=1)

    acc[...] = jnp.zeros_like(acc)

    def splat(scalar, shape):
        return jnp.full(shape, scalar.astype(jnp.float32)).astype(jnp.bfloat16)

    def product(left, j):
        total = None
        deep = 2 * BLOCK if feats % (2 * BLOCK) == 0 else BLOCK
        for lo in range(0, feats, deep):
            tall = []
            for b in range(lo // BLOCK, (lo + deep) // BLOCK):
                wide = []
                for n in range(2 * width // BLOCK):
                    mask = gate_m if n < width // BLOCK else up_m
                    keep = mask[b, j * (width // BLOCK) + n % (width // BLOCK)]
                    wide.append(wgu[j, b * BLOCK:(b + 1) * BLOCK, n * BLOCK:(n + 1) * BLOCK] * splat(keep, (BLOCK, BLOCK)))
                tall.append(jnp.concatenate(wide, axis=1))
            piece = jnp.dot(left[:, lo:lo + deep], jnp.concatenate(tall, axis=0), preferred_element_type=jnp.float32)
            total = piece if total is None else total + piece
        return total

    def ahead(d):
        return z + 1 - 2 * d

    def behind(d):
        return z - 1 + 2 * d

    def part_copy(d, u, m):
        return pltpu.make_async_remote_copy(
            src_ref=part.at[d, u, m], dst_ref=taken.at[d, u, m],
            send_sem=part_send.at[d, u, m], recv_sem=part_recv.at[d, u, m],
            device_id={"feat": ahead(d)}, device_id_type=MESH)

    heads = min(HEADS, down_chunks, early) if nr == 2 and nf > 1 else 0
    own_copy.wait()
    for copy in mask_copies:
        copy.wait()
    side = (z > 0).astype(jnp.int32)

    def head(c):
        @pl.when((z == 0) | (z == nf - 1))
        def _():
            j = side * up_chunks + c
            gate_copy(j).wait()
            up_copy(j).wait()
            part[side, c, 0] = product(arrived[(nx - 1) * nr + r], j).astype(jnp.bfloat16)

    def send_head(c):
        @pl.when((z == 0) | (z == nf - 1))
        def _():
            part_copy(side, c, 0).start()

    if heads:
        head(0)

    ends = (z == 0).astype(jnp.int32) + (z == nf - 1).astype(jnp.int32)
    pl.semaphore_wait(barrier, nx * nr + 1 - ends)

    def near_copy(step):
        return pltpu.make_async_remote_copy(
            src_ref=tokens, dst_ref=arrived.at[(nx - 1) * nr + r],
            send_sem=tok_send.at[(nx - 1) * nr + step], recv_sem=tok_recv.at[(nx - 1) * nr + r],
            device_id={"rep": lax.rem(r + step, nr)}, device_id_type=MESH)

    def far_copy(g, q):
        slot = (nx - 2 - g) * nr + r
        return pltpu.make_async_remote_copy(
            src_ref=tokens, dst_ref=arrived.at[slot],
            send_sem=tok_send.at[g * nr + q], recv_sem=tok_recv.at[slot],
            device_id={"tok": chip(g), "rep": q}, device_id_type=MESH)

    def landed(slot):
        pltpu.make_async_remote_copy(
            src_ref=tokens, dst_ref=arrived.at[slot],
            send_sem=tok_send.at[0], recv_sem=tok_recv.at[slot],
            device_id={"rep": lax.rem(r + 1, nr)}, device_id_type=MESH).wait_recv()

    if heads:
        send_head(0)
    for step in range(1, nr):
        near_copy(step).start()
    for g in range(nx - 1):
        for q in range(nr):
            far_copy(g, q).start()

    if heads:
        @pl.loop(1, heads)
        def _(c):
            head(c)
            send_head(c)

    for step in range(1, nr):
        landed((nx - 1) * nr + lax.rem(r + step, nr))
    for q in range(nr):
        tok[nx - 1, q * rows:(q + 1) * rows, :] = arrived[(nx - 1) * nr + q]

    def place(d):
        p = jnp.where(d == 0, z, nf - 1 - z)
        count = up_chunks if up_chunks == down_chunks else jnp.where(d == 0, up_chunks, down_chunks)
        return p, count, nx * count

    def unit(u, d, count):
        mine = (u < early) | (u >= early + (nx - 1) * count)
        other = jnp.maximum(u - early, 0)
        group = jnp.where(mine, nx - 1, other // count)
        c = jnp.where(u < early, u, jnp.where(mine, u - (nx - 1) * count, other % count))
        first = (u < early) | ((u >= 2 * early) & (u < early + count))
        return group, d * up_chunks + c, first

    def hidden_unit(h, count):
        others = (nx - 1) * count
        c = h - others
        return jnp.where(c < 0, early + h, jnp.where(c < early, c, h))

    def hid_copy(d, u):
        return pltpu.make_async_remote_copy(
            src_ref=hid.at[d, u], dst_ref=hid.at[d, u],
            send_sem=hid_send.at[d, u], recv_sem=hid_recv.at[d, u],
            device_id={"feat": behind(d)}, device_id_type=MESH)

    others = (nx - 1) * up_chunks
    begin = HOP * (nf - 1) + max(nr * (early + others) - others, (nr - 1) * nx * up_chunks) + SLACK

    def prepare(k, d):
        p, count, units = place(d)
        t = k - HOP * p + nr + nr * lead
        c = t // nr

        @pl.when((t >= 0) & (c < count) & (t % nr == 0))
        def _():
            gate_copy(d * up_chunks + c).start(priority=1)
            up_copy(d * up_chunks + c).start(priority=1)

    def multiply(k, d):
        p, count, units = place(d)
        t = k - HOP * p + nr
        u = t // nr

        @pl.when((t >= 0) & (u < units) & (t % nr == 0))
        def _():
            group, j, first = unit(u, d, count)

            below = u - (count - lead if nx > 1 else 0)

            @pl.when((below >= 0) & (below < count))
            def _():
                down_copy(d * up_chunks + below).start(priority=1)

            @pl.when(first & ((p > 0) | (u >= heads)))
            def _():
                gate_copy(j).wait()
                up_copy(j).wait()

            total = product(tok[group], j)
            for m in range(nr):
                sums[d, u % 2, m] = total[m * rows:(m + 1) * rows, :]

    def reduce(k, d):
        p, count, units = place(d)
        t = k - HOP * p
        u, m = t // nr, t % nr
        if heads == 2:
            u, m = jnp.where(t < 4, t % 2, u), jnp.where(t < 4, t // 2, m)
        block = (r + m) % nr

        @pl.when((t >= jnp.where(p == 0, heads, 0)) & (u < units))
        def _():
            here = sums.at[d, u % 2, block]

            @pl.when(p > 0)
            def _():
                part_copy(d, u, m).wait_recv()
                here[...] += taken[d, u, m].astype(jnp.float32)

            @pl.when(p < nf - 1)
            def _():
                part[d, u, m] = here[...].astype(jnp.bfloat16)
                part_copy(d, u, m).start()

            for s in range(nr):
                @pl.when((p == nf - 1) & (block == s))
                def _():
                    gate, up = here[:, :width], here[:, width:]
                    hid[d, u, s * rows:(s + 1) * rows, :] = (gate / (1.0 + jnp.exp(-gate)) * up).astype(jnp.bfloat16)

    def lower(d, u, group, j, n):
        cols = slice(2 * n * BLOCK, 2 * (n + 1) * BLOCK)
        tall = []
        for b in range(width // BLOCK):
            wide = []
            for m in (2 * n, 2 * n + 1):
                keep = down_m[m, j * (width // BLOCK) + b]
                wide.append(wd[j, b * BLOCK:(b + 1) * BLOCK, m * BLOCK:(m + 1) * BLOCK] * splat(keep, (BLOCK, BLOCK)))
            tall.append(jnp.concatenate(wide, axis=1))
        acc[group, :, cols] += jnp.dot(hid[d, u], jnp.concatenate(tall, axis=0), preferred_element_type=jnp.float32)

    def pass_on(h, d):
        p, count, units = place(d)
        u = hidden_unit(h, count)
        group, j, _ = unit(u, d, count)

        @pl.when(p < nf - 1)
        def _():
            hid_copy(d, u).wait_recv()

        @pl.when(p > 0)
        def _():
            hid_copy(d, u).start()

        @pl.when(h < count)
        def _():
            down_copy(j).wait()

        return u, group, j

    flip = (z > nf - 1 - z).astype(jnp.int32)

    def spread(k, d):
        p, count, units = place(d)
        h = k - begin - BACK * (nf - 1 - p)

        @pl.when((h >= 0) & (h < units - (d == flip).astype(jnp.int32)))
        def _():
            u, group, j = pass_on(h, d)
            for n in range(feats // (2 * BLOCK)):
                lower(d, u, group, j, n)

    def cross_copy(g, step):
        return pltpu.make_async_remote_copy(
            src_ref=shared.at[g, step], dst_ref=crossed.at[g, r],
            send_sem=cross_send.at[g, step], recv_sem=cross_recv.at[g, r],
            device_id={"rep": lax.rem(r + step, nr)}, device_id_type=MESH)

    def crossing(g, q):
        return pltpu.make_async_remote_copy(
            src_ref=shared.at[g, 0], dst_ref=crossed.at[g, q],
            send_sem=cross_send.at[g, 0], recv_sem=cross_recv.at[g, q],
            device_id={"rep": lax.rem(r + 1, nr)}, device_id_type=MESH)

    def out_copy(g):
        return pltpu.make_async_remote_copy(
            src_ref=leaving.at[g], dst_ref=coming.at[g],
            send_sem=out_send.at[g], recv_sem=out_recv.at[g],
            device_id={"tok": chip(g)}, device_id_type=MESH)

    def row_block(q):
        return pl.ds(pl.multiple_of(q * rows, 8), rows)

    def last_copy(step, n):
        cols = pl.ds(n * tail, tail)
        return pltpu.make_async_remote_copy(
            src_ref=ending.at[step, :, cols], dst_ref=ended.at[r, :, cols],
            send_sem=end_send.at[step, n], recv_sem=end_recv.at[r, n],
            device_id={"rep": lax.rem(r + step, nr)}, device_id_type=MESH)

    def last_landed(q, n):
        cols = pl.ds(n * tail, tail)
        pltpu.make_async_remote_copy(
            src_ref=ending.at[0, :, cols], dst_ref=ended.at[q, :, cols],
            send_sem=end_send.at[0, n], recv_sem=end_recv.at[q, n],
            device_id={"rep": lax.rem(r + 1, nr)}, device_id_type=MESH).wait_recv()

    starts = HOP * jnp.minimum(z, nf - 1 - z) + nr * early - nr
    @pl.loop(-nr, begin + BACK * (nf - 1) + nx * up_chunks)
    def _(k):
        @pl.loop(0, 2)
        def _(e):
            reduce(k, (e + flip) % 2)

        @pl.when(k == starts)
        def _():
            for g in range(nx - 1):
                for q in range(nr):
                    landed(g * nr + q)
                    tok[g, q * rows:(q + 1) * rows, :] = arrived[g * nr + q]

        @pl.loop(0, 2)
        def _(e):
            prepare(k, (e + flip) % 2)
            multiply(k, (e + flip) % 2)

        @pl.loop(0, 2)
        def _(e):
            spread(k, (e + flip) % 2)

        for g in range(nx - 1):
            ends = [begin + BACK * (nf - 1 - p) + (g + 1) * count - 1
                    for count, p in ((up_chunks, z), (down_chunks, nf - 1 - z))]

            @pl.when(k == jnp.maximum(*ends))
            def _():
                for step in range(1, nr):
                    shared[g, step] = acc[g, row_block(lax.rem(r + step, nr)), :].astype(jnp.bfloat16)
                    cross_copy(g, step).start()

            @pl.when(k == jnp.maximum(*ends) + PAUSE)
            def _():
                total = acc[g, row_block(r), :]
                for step in range(1, nr):
                    q = lax.rem(r + step, nr)
                    crossing(g, q).wait_recv()
                    total += crossed[g, q].astype(jnp.float32)
                leaving[g] = total.astype(jnp.bfloat16)
                out_copy(g).start()

    for step in range(1, nr):
        near_copy(step).wait_send()
    for g in range(nx - 1):
        for q in range(nr):
            far_copy(g, q).wait_send()

    @pl.loop(0, 2)
    def _(d):
        p, count, units = place(d)

        @pl.loop(0, nx * up_chunks)
        def _(u):
            @pl.when((u < units) & (p < nf - 1))
            def _():
                for m in range(nr):
                    part_copy(d, u, m).wait_send()

    _, _, last_units = place(flip)
    u, group, j = pass_on(last_units - 1, flip)
    for n in range(feats // tail):
        for b in range(tail // (2 * BLOCK)):
            lower(flip, u, nx - 1, j, n * (tail // (2 * BLOCK)) + b)
        cols = slice(n * tail, (n + 1) * tail)
        for step in range(1, nr):
            ending[step, :, cols] = acc[nx - 1, row_block(lax.rem(r + step, nr)), cols].astype(jnp.bfloat16)
            last_copy(step, n).start()

    for g in range(nx - 1):
        for step in range(1, nr):
            cross_copy(g, step).wait_send()
        out_copy(g).wait_send()

    @pl.loop(0, 2)
    def _(d):
        p, count, units = place(d)

        @pl.loop(0, nx * up_chunks)
        def _(u):
            @pl.when((u < units) & (p > 0))
            def _():
                hid_copy(d, u).wait_send()

    own = row_block(r)
    for g in range(nx - 1):
        pltpu.make_async_remote_copy(
            src_ref=leaving.at[0], dst_ref=coming.at[g],
            send_sem=out_send.at[0], recv_sem=out_recv.at[g],
            device_id={"rep": lax.rem(r + 1, nr)}, device_id_type=MESH).wait_recv()
        acc[nx - 1, own, :] += coming[g].astype(jnp.float32)
    for n in range(feats // tail):
        cols = slice(n * tail, (n + 1) * tail)
        final = acc[nx - 1, own, cols]
        for step in range(1, nr):
            q = lax.rem(r + step, nr)
            last_landed(q, n)
            final += ended[q, :, cols].astype(jnp.float32)
        out[:, cols] = final.astype(out.dtype)

    for step in range(1, nr):
        for n in range(feats // tail):
            last_copy(step, n).wait_send()


def solution(mesh):
    nf, nx, nr = mesh.shape["feat"], mesh.shape["tok"], mesh.shape["rep"]

    def shards(tokens, gate_weight, up_weight, down_weight, gate_mask, up_mask, down_mask):
        rows, feats = tokens.shape
        hidden = gate_weight.shape[1]
        width = 2 * BLOCK if hidden % (4 * BLOCK) == 0 else BLOCK
        chunks = hidden // width
        units = nx * ((chunks + 1) // 2)
        high = nr * rows
        pieces = feats // (TAIL if feats % TAIL == 0 else 2 * BLOCK)
        bf16, f32 = jnp.bfloat16, jnp.float32
        dma = pltpu.SemaphoreType.DMA
        hbm = pl.BlockSpec(memory_space=pl.ANY)
        return pl.pallas_call(
            functools.partial(kernel, nf, nx, nr),
            out_shape=pltpu.VMEM((rows, feats), bf16),
            in_specs=[hbm] * 7,
            out_specs=pl.BlockSpec(memory_space=pltpu.VMEM),
            scratch_shapes=[
                pltpu.VMEM((nx * nr, rows, feats), bf16),
                pltpu.VMEM((nx, high, feats), bf16),
                pltpu.VMEM((chunks, feats, 2 * width), bf16),
                pltpu.VMEM((chunks, width, feats), bf16),
                pltpu.VMEM((2, 2, nr, rows, 2 * width), f32),
                pltpu.VMEM((2, units, nr, rows, 2 * width), bf16),
                pltpu.VMEM((2, units, nr, rows, 2 * width), bf16),
                pltpu.VMEM((2, units, high, width), bf16),
                pltpu.VMEM((nx, high, feats), f32),
                pltpu.VMEM((max(nx - 1, 1), rows, feats), bf16),
                pltpu.VMEM((max(nx - 1, 1), rows, feats), bf16),
                pltpu.VMEM((max(nx - 1, 1), nr, rows, feats), bf16),
                pltpu.VMEM((max(nx - 1, 1), nr, rows, feats), bf16),
                pltpu.VMEM((nr, rows, feats), bf16),
                pltpu.VMEM((nr, rows, feats), bf16),
                pltpu.SMEM(gate_mask.shape, jnp.int32), pltpu.SMEM(up_mask.shape, jnp.int32),
                pltpu.SMEM(down_mask.shape[::-1], jnp.int32),
                dma((nx * nr,)), dma((nx * nr,)), dma(()),
                dma((chunks,)), dma((chunks,)), dma((chunks,)),
                dma((2, units, nr)), dma((2, units, nr)), dma((2, units)), dma((2, units)),
                dma((max(nx - 1, 1),)), dma((max(nx - 1, 1),)),
                dma((max(nx - 1, 1), nr)), dma((max(nx - 1, 1), nr)),
                dma((nr, pieces)), dma((nr, pieces)), dma((3,)),
            ],
            compiler_params=pltpu.CompilerParams(
                collective_id=0, has_side_effects=True, vmem_limit_bytes=63 * 1024 * 1024),
        )(tokens, gate_weight, up_weight, down_weight, gate_mask, up_mask, down_mask.T)

    return jax.shard_map(
        shards,
        mesh=mesh,
        in_specs=(
            P(("groups", "tok", "rep"), "feat"),
            P("feat", ("tok", "rep")),
            P("feat", ("tok", "rep")),
            P(("tok", "rep"), "feat"),
            P("feat", ("tok", "rep")),
            P("feat", ("tok", "rep")),
            P(("tok", "rep"), "feat"),
        ),
        out_specs=P(("groups", "tok", "rep"), "feat"),
        check_vma=False,
    )
```
